32 devices in a mesh: grp: 2 (over x), lon: 16 (over z, y, core).
Axes of the slice: x: 2, y: 2, z: 4, core: 2. Of those that a mesh axis runs over, the one named last changes fastest.
Arguments:
- tracer_pert: float32 [4, 50, 32, 1024], P('grp', None, 'lon'), parts along dimension 0, may hold values from -60 to 60
- surface_pert: float32 [4, 32, 1024], P('grp', 'lon'), parts along dimension 0, may hold values from -60 to 60
- zonal_flow: float32 [50, 32, 1024], P(None, 'lon'), may hold values from -3.2 to 3.2
- merid_flow: float32 [50, 32, 1024], P(None, 'lon'), may hold values from -3.2 to 3.2
- bottom_level: int32 [32, 1024], P('lon'), may hold values from 0 to 50
Outputs:
- tracer_vec: float32 [4, 50, 32, 1024], P('grp', None, 'lon'), parts along dimension 0
- surface_vec: float32 [4, 32, 1024], P('grp', 'lon'), parts along dimension 0
- growth: float32 [6], P('grp'), parts along dimension 0
The draws below stay inside these ranges and needn't reach their ends.
There are 2 independent parts, one for each index of `grp`. The reference program is written for one: setup_inputs(seed, part) draws one part's arguments, and reference() takes and returns one part's arrays. A program takes and returns all parts, laid end to end along the dimension named above; an argument that names none is the same for every part. Nothing has to cross between parts.
Inputs may be any that keep to these rules, and one draw needn't show every extreme that they name: `bottom_level`: 0 marks a land column, 50 a column wet to the bottom level.
All inputs are finite; a program needn't handle non-finite values.
Results may differ from the reference program's by a relative error of at most 0.0001.
Values sent between devices are 32-bit elements; how exact they have to be, the bound alone decides.
A program may use at most 64 MiB of HBM per device.

```python
import jax
import jax.numpy as jnp
from jax import lax

NV = 2
NZ = 50
NY = 1024
NSUB = 2
ITERS = 3
NX = 32


def shaped_field(key, shape):
    key_base, key_rough, key_rows = jax.random.split(key, 3)
    base = jnp.clip(jax.random.normal(key_base, shape, jnp.float32), -4.0, 4.0)
    mixed = jnp.concatenate([base[:1], 0.6 * base[:1] + 0.8 * base[1:]], axis=0)
    envelope = 0.5 + 1.5 * jnp.arange(NX, dtype=jnp.float32) / NX
    rough = jnp.exp(jax.random.uniform(key_rough, shape, jnp.float32, -0.5, 0.5))
    row_scale = jnp.exp(jax.random.uniform(key_rows, (NY,), jnp.float32, -1.15, 1.15))
    return mixed * envelope[:, None] * rough * row_scale


def draw_tracer_pert(key, part):
    return shaped_field(jax.random.fold_in(key, 11), (NV, NZ, NX, NY))


def draw_surface_pert(key, part):
    return shaped_field(jax.random.fold_in(key, 23), (NV, NX, NY))


def touch_ends(drawn, key, least, largest):
    longest = drawn.shape.index(max(drawn.shape))
    spots = []
    for shift in (0, 1):
        where = [jax.random.randint(jax.random.fold_in(key, axis), (), 0, length) for axis, length in enumerate(drawn.shape)]
        where[longest] = (where[longest] + shift) % drawn.shape[longest]
        spots.append(tuple(where))
    return drawn.at[spots[0]].set(least).at[spots[1]].set(largest)


def level_of(rng, dims, shards, low, high):
    factor_of = 1.0
    for position, shards_of in shards:
        steps = jax.random.uniform(jax.random.fold_in(jax.random.fold_in(rng, 6), position), (shards_of,), jnp.float32, low / len(shards), high / len(shards))
        factor_of = factor_of * jnp.repeat(jnp.exp(steps), dims[position] // shards_of).reshape((-1,) + (1,) * (len(dims) - 1 - position))
    return factor_of


def scatter_about(own_key, shape, deviation, bound, cuts=(), held_as=jnp.bfloat16):
    array = deviation * jax.random.normal(own_key, shape, jnp.float32)
    if cuts:
        array = array * level_of(own_key, shape, cuts, -0.22, 0.18)
    return jnp.clip(array, -bound, bound).astype(held_as)


def setup_inputs(seed: int = 0, part: int = 0) -> dict:
    seeds = jax.random.split(jax.random.key(seed), 6)
    part_splits = jax.random.split(jax.random.fold_in(seeds[5], part), 6)
    return {
        "tracer_pert": draw_tracer_pert(jax.random.fold_in(jax.random.fold_in(seeds[5], part), 71), part),
        "surface_pert": draw_surface_pert(jax.random.fold_in(jax.random.fold_in(seeds[5], part), 71), part),
        "zonal_flow": scatter_about(seeds[2], (NZ, NX, NY), 0.8, 3.2, ((1, 16),), jnp.float32),
        "merid_flow": scatter_about(seeds[3], (NZ, NX, NY), 0.8, 3.2, ((1, 16),), jnp.float32),
        "bottom_level": touch_ends(jax.random.randint(seeds[4], (NX, NY), 0, NZ + 1), jax.random.fold_in(seeds[4], 1), 0, NZ).astype(jnp.int32),
    }


DIFFUSIVITY = 0.5
TIME_STEP = 0.2
SURFACE_COUPLING = 0.5
STERIC_GAIN = 2.0
EPSILON = 1e-06

def tracer_update(tracer, zonal_flow, merid_flow, wet_cells):
    east_vals = jnp.roll(tracer, -1, axis=2)
    face_x = wet_cells * jnp.roll(wet_cells, -1, axis=1)
    flow_x = 0.5 * (zonal_flow + jnp.roll(zonal_flow, -1, axis=1))
    flux_x = face_x * (0.5 * flow_x * (tracer + east_vals) - DIFFUSIVITY * (east_vals - tracer))
    div_x = flux_x - jnp.roll(flux_x, 1, axis=2)
    face_y = wet_cells[..., :-1] * wet_cells[..., 1:]
    flow_y = 0.5 * (merid_flow[..., :-1] + merid_flow[..., 1:])
    flux_y = face_y * (0.5 * flow_y * (tracer[..., :-1] + tracer[..., 1:]) - DIFFUSIVITY * (tracer[..., 1:] - tracer[..., :-1]))
    padded = jnp.pad(flux_y, ((0, 0), (0, 0), (0, 0), (1, 1)))
    div_y = padded[..., 1:] - padded[..., :-1]
    return tracer - TIME_STEP * (div_x + div_y)

def surface_operator(surface, face_x, face_y):
    grad_x = face_x * (jnp.roll(surface, -1, axis=1) - surface)
    lap_x = grad_x - jnp.roll(grad_x, 1, axis=1)
    grad_y = face_y * (surface[..., 1:] - surface[..., :-1])
    padded = jnp.pad(grad_y, ((0, 0), (0, 0), (1, 1)))
    lap_y = padded[..., 1:] - padded[..., :-1]
    return surface - SURFACE_COUPLING * (lap_x + lap_y)

def reference(tracer_pert, surface_pert, zonal_flow, merid_flow, bottom_level):
    levels = jnp.arange(NZ, dtype=jnp.int32)[:, None, None]
    wet_cells = (levels < bottom_level[None]).astype(jnp.float32)
    depths = bottom_level.astype(jnp.float32)
    tracer = wet_cells[None] * tracer_pert
    for substep in range(NSUB):
        tracer = tracer_update(tracer, zonal_flow, merid_flow, wet_cells)
    height = surface_pert * (depths > 0).astype(jnp.float32)[None]
    forcing = height + STERIC_GAIN * lax.optimization_barrier(jnp.sum(tracer, axis=1)) / NZ
    face_x = jnp.minimum(depths, jnp.roll(depths, -1, axis=0))
    face_y = jnp.minimum(depths[:, :-1], depths[:, 1:])
    solution = height
    residual = forcing - surface_operator(height, face_x, face_y)
    direction = residual
    norm_now = lax.optimization_barrier(jnp.sum(residual * residual, axis=(1, 2)))
    for iteration in range(ITERS):
        image_vec = surface_operator(direction, face_x, face_y)
        step_size = norm_now / lax.optimization_barrier(jnp.sum(direction * image_vec, axis=(1, 2)))
        solution = solution + step_size[:, None, None] * direction
        residual = residual - step_size[:, None, None] * image_vec
        if iteration + 1 < ITERS:
            norm_next = lax.optimization_barrier(jnp.sum(residual * residual, axis=(1, 2)))
            direction = residual + (norm_next / norm_now)[:, None, None] * direction
            norm_now = norm_next
    cell_count = (NZ + 1) * NX * NY

    def inner_product(tracer_a, surface_a, tracer_b, surface_b):
        return (jnp.sum(tracer_a * tracer_b) + jnp.sum(surface_a * surface_b)) / cell_count
    first_tracer, second_tracer = (tracer[0], tracer[1])
    first_surface, second_surface = (solution[0], solution[1])
    scale_one = jnp.sqrt(inner_product(first_tracer, first_surface, first_tracer, first_surface) + EPSILON)
    unit_tracer = first_tracer / scale_one
    unit_surface = first_surface / scale_one
    cross = inner_product(second_tracer, second_surface, unit_tracer, unit_surface)
    rest_tracer = second_tracer - cross * unit_tracer
    rest_surface = second_surface - cross * unit_surface
    scale_two = jnp.sqrt(inner_product(rest_tracer, rest_surface, rest_tracer, rest_surface) + EPSILON)
    tracer_vec = jnp.stack([unit_tracer, rest_tracer / scale_two])
    surface_vec = jnp.stack([unit_surface, rest_surface / scale_two])
    growth = jnp.stack([scale_one, cross, scale_two])
    return (tracer_vec, surface_vec, growth)
```

```python
import functools

import jax
import jax.numpy as jnp
from jax import lax
from jax.experimental import pallas as pl
from jax.experimental.pallas import tpu as pltpu
from jax.sharding import PartitionSpec as P

DIFFUSIVITY = 0.5
TIME_STEP = 0.2
SURFACE_COUPLING = 0.5
STERIC_GAIN = 2.0
EPSILON = 1e-06
MESH = pl.DeviceIdType.MESH
CHUNKS = 5
UNROLL = 2
REACH = 2


def chunk_bounds(levels):
    count = min(CHUNKS, levels)
    edges = [levels * i // count for i in range(count + 1)]
    return list(zip(edges[:-1], edges[1:]))


def peers_loop(n, body):
    if n <= 16:
        for i in range(1, n):
            body(i)
    else:

        def step(i, carry):
            body(i)
            return carry

        lax.fori_loop(1, n, step, 0)


def kernel(
    n, trc, surf, zon, mer, bot, out, sout, gout,
    s_a, r_a, s_b, r_b, coef, stat, ster, pack, red,
    a_send, a_recv, b_send, b_recv, st_send, st_recv, se_send, se_recv, rd_send, rd_recv,
):
    me = lax.axis_index("lon")
    levels = zon.shape[0]
    chunks = chunk_bounds(levels)
    right, left = lax.rem(me + 1, n), lax.rem(me + n - 1, n)
    side_dev = (left, right)
    tile = (8, 128)
    lane = lax.broadcasted_iota(jnp.int32, tile, 1)
    row = lax.broadcasted_iota(jnp.int32, tile, 0)
    last_lane, first_lane = lane == 127, lane == 0

    def north(x):
        rolled = pltpu.roll(x, 127, 1)
        return jnp.where(last_lane, pltpu.roll(rolled, 7, 0), rolled)

    def south(x):
        rolled = pltpu.roll(x, 1, 1)
        return jnp.where(first_lane, pltpu.roll(rolled, 1, 0), rolled)

    def col(c):
        return pl.ds(c, 8, stride=2)

    barrier = pltpu.get_barrier_semaphore()

    def greet(i):
        pl.semaphore_signal(
            barrier, inc=1, device_id={"lon": lax.rem(me + i, n)}, device_id_type=MESH
        )

    peers_loop(n, greet)

    for c in range(2):
        d = bot[col(c), :].astype(jnp.float32)
        stat[REACH, 4 + c] = d
        for v in range(2):
            stat[REACH, 2 * v + c] = jnp.where(d > 0, surf[v, col(c), :], 0.0)

    def gather_chunk(k0, k1):
        def step(k, carry):
            for c in range(2):
                s_a[c, k, 0] = trc[0, k, col(c), :]
                s_a[c, k, 1] = trc[1, k, col(c), :]
                s_a[c, k, 2] = zon[k, col(c), :]
            return carry

        lax.fori_loop(k0, k1, step, 0, unroll=UNROLL)

    def a_copy(g, side):
        k0, k1 = chunks[g]
        return pltpu.make_async_remote_copy(
            src_ref=s_a.at[side, pl.ds(k0, k1 - k0)],
            dst_ref=r_a.at[1 - side, pl.ds(k0, k1 - k0)],
            send_sem=a_send.at[side, g],
            recv_sem=a_recv.at[1 - side, g],
            device_id={"lon": side_dev[side]},
            device_id_type=MESH,
        )

    def b_copy(g, side):
        k0, k1 = chunks[g]
        return pltpu.make_async_remote_copy(
            src_ref=s_b.at[side, pl.ds(k0, k1 - k0)],
            dst_ref=r_b.at[1 - side, pl.ds(k0, k1 - k0)],
            send_sem=b_send.at[side, g],
            recv_sem=b_recv.at[1 - side, g],
            device_id={"lon": side_dev[side]},
            device_id_type=MESH,
        )

    shifts = [s for s in range(-REACH, REACH + 1) if s != 0]
    shifts.sort(key=abs)

    def halo_copy(buf, send, recv, s):
        return pltpu.make_async_remote_copy(
            src_ref=buf.at[REACH],
            dst_ref=buf.at[REACH - s],
            send_sem=send.at[REACH - s],
            recv_sem=recv.at[REACH - s],
            device_id={"lon": lax.rem(me + s + n, n)},
            device_id_type=MESH,
        )

    gather_chunk(*chunks[0])
    pl.semaphore_wait(barrier, n - 1)
    for s in shifts:
        halo_copy(stat, st_send, st_recv, s).start()
    for side in range(2):
        a_copy(0, side).start()
    for g in range(1, len(chunks)):
        gather_chunk(*chunks[g])
        for side in range(2):
            a_copy(g, side).start()

    for s in shifts:
        halo_copy(stat, st_send, st_recv, s).wait_recv()
    width = 2 * (2 * REACH + 1)
    mid = 2 * REACH

    def depth(i):
        return stat[i // 2, 4 + i % 2]

    def height(v, i):
        return stat[i // 2, 2 * v + i % 2]

    def y_face(i):
        d = depth(i)
        wall = jnp.logical_and(last_lane, row == 7)
        return jnp.where(wall, 0.0, jnp.minimum(d, north(d)))

    def x_face(i):
        return jnp.minimum(depth(i), depth(i + 1))

    half = TIME_STEP * 0.25
    diff = TIME_STEP * DIFFUSIVITY

    for g, (k0, k1) in enumerate(chunks):
        for side in range(2):
            a_copy(g, side).wait_recv()

        def first(k, carry):
            kf = k.astype(jnp.float32)
            z = (r_a[0, k, 2], s_a[0, k, 2], s_a[1, k, 2], r_a[1, k, 2])
            cx = []
            for f in range(3):
                open_f = kf < x_face(mid - 1 + f)
                u = half * (z[f] + z[f + 1])
                cx.append((jnp.where(open_f, u + diff, 0.0), jnp.where(open_f, u - diff, 0.0)))
            cy = []
            for c in range(2):
                open_f = kf < faces_y[c]
                m = mer[k, col(c), :]
                u = half * (m + north(m))
                cy.append((jnp.where(open_f, u + diff, 0.0), jnp.where(open_f, u - diff, 0.0)))
            for q, (lo, hi) in enumerate(cx + cy):
                coef[k, 2 * q] = lo
                coef[k, 2 * q + 1] = hi
            wet = [kf < depth(mid + c) for c in range(2)]
            for v in range(2):
                t = (
                    r_a[0, k, v],
                    jnp.where(wet[0], s_a[0, k, v], 0.0),
                    jnp.where(wet[1], s_a[1, k, v], 0.0),
                    r_a[1, k, v],
                )
                fx = [cx[f][0] * t[f] + cx[f][1] * t[f + 1] for f in range(3)]
                for c in range(2):
                    fy = cy[c][0] * t[c + 1] + cy[c][1] * north(t[c + 1])
                    s_b[c, k, v] = t[c + 1] - ((fx[c + 1] - fx[c]) + (fy - south(fy)))
            return carry

        if g == 0:
            faces_y = [y_face(mid + c) for c in range(2)]
        lax.fori_loop(k0, k1, first, 0, unroll=UNROLL)
        for side in range(2):
            b_copy(g, side).start()

    face_x = {i: SURFACE_COUPLING * x_face(i) for i in range(0, width - 1)}
    face_y = {i: SURFACE_COUPLING * y_face(i) for i in range(1, width - 1)}

    def lap(s, cols):
        gx = {i: face_x[i] * (s[i + 1] - s[i]) for i in range(cols[0] - 1, cols[-1] + 1)}
        res = {}
        for i in cols:
            gy = face_y[i] * (north(s[i]) - s[i])
            res[i] = -((gx[i] - gx[i - 1]) + (gy - south(gy)))
        return res

    lap_h = [
        lap({i: height(v, i) for i in range(width)}, range(1, width - 1)) for v in range(2)
    ]

    zero = jnp.zeros(tile, jnp.float32)
    totals = (zero,) * 7
    for g, (k0, k1) in enumerate(chunks):
        for side in range(2):
            b_copy(g, side).wait_recv()

        def second(k, carry):
            sums, grams = list(carry[:4]), list(carry[4:])
            cx = [(coef[k, 2 * f], coef[k, 2 * f + 1]) for f in range(3)]
            cy = [(coef[k, 6 + 2 * c], coef[k, 7 + 2 * c]) for c in range(2)]
            new = []
            for v in range(2):
                t = (r_b[0, k, v], s_b[0, k, v], s_b[1, k, v], r_b[1, k, v])
                fx = [cx[f][0] * t[f] + cx[f][1] * t[f + 1] for f in range(3)]
                for c in range(2):
                    fy = cy[c][0] * t[c + 1] + cy[c][1] * north(t[c + 1])
                    val = t[c + 1] - ((fx[c + 1] - fx[c]) + (fy - south(fy)))
                    out[v, k, col(c), :] = val
                    sums[2 * v + c] = sums[2 * v + c] + val
                    new.append(val)
            grams[0] = grams[0] + (new[0] * new[0] + new[1] * new[1])
            grams[1] = grams[1] + (new[0] * new[2] + new[1] * new[3])
            grams[2] = grams[2] + (new[2] * new[2] + new[3] * new[3])
            return tuple(sums + grams)

        totals = lax.fori_loop(k0, k1, second, totals, unroll=UNROLL)

    for q in range(4):
        ster[REACH, q] = totals[q]
    for s in shifts:
        halo_copy(ster, se_send, se_recv, s).start()

    def total_of(x):
        return jnp.sum(jnp.sum(x, axis=1, keepdims=True), axis=0, keepdims=True)

    def red_copy(turn, i):
        return pltpu.make_async_remote_copy(
            src_ref=pack.at[turn],
            dst_ref=red.at[turn, me],
            send_sem=rd_send.at[turn],
            recv_sem=rd_recv.at[turn],
            device_id={"lon": lax.rem(me + i, n)},
            device_id_type=MESH,
        )

    def all_sum(turn, parts):
        mine = zero
        for q, part in enumerate(parts):
            mine = jnp.where(lane == q, total_of(part), mine)
        pack[turn] = mine
        red[turn, me] = mine
        peers_loop(n, lambda i: red_copy(turn, i).start())
        every = pltpu.make_async_copy(
            red.at[turn, pl.ds(0, n - 1)], red.at[turn, pl.ds(0, n - 1)], rd_recv.at[turn]
        )
        every.wait()
        terms = [red[turn, i] for i in range(n)]
        while len(terms) > 1:
            terms = [
                terms[i] + terms[i + 1] if i + 1 < len(terms) else terms[i]
                for i in range(0, len(terms), 2)
            ]
        return [terms[0][0:1, q : q + 1] for q in range(len(parts))]

    gram_parts = list(totals[4:])
    for s in shifts:
        halo_copy(ster, se_send, se_recv, s).wait_recv()

    own = (mid, mid + 1)

    def dot(a, b):
        return a[own[0]] * b[own[0]] + a[own[1]] * b[own[1]]

    gain = STERIC_GAIN / levels
    res, lres, llres, parts = [], [], [], []
    for v in range(2):
        r = {
            i: gain * ster[i // 2, 2 * v + i % 2] - lap_h[v][i] for i in range(1, width - 1)
        }
        lr = lap(r, range(2, width - 2))
        llr = lap(lr, range(own[0], own[1] + 1))
        res.append(r)
        lres.append(lr)
        parts += [dot(r, r), dot(r, lr), dot(lr, lr), dot(lr, llr)]
    sums = all_sum(0, parts + gram_parts)
    gram_t = sums[8:]

    sol, dir1, res2, rr1s, parts = [], [], [], [], []
    ldir1s = []
    for v in range(2):
        l0, l1, l2, l3 = sums[4 * v : 4 * v + 4]
        step0 = l0 / (l0 + l1)
        ratio = l1 / l0
        rr1 = step0 * step0 * jnp.maximum(l2 - l1 * ratio, 0.0)
        beta0 = rr1 / l0
        along = step0 * ratio + beta0
        p1ap1 = (
            along * along * (l0 + l1)
            - 2.0 * along * step0 * (l1 + l2)
            + step0 * step0 * (l2 + l3)
        )
        step1 = rr1 / p1ap1
        r, lr = res[v], lres[v]
        p1 = {i: along * r[i] - step0 * lr[i] for i in range(own[0] - 2, own[1] + 3)}
        lp1 = lap(p1, range(own[0] - 1, own[1] + 2))
        r2 = {
            i: step0 * (ratio * r[i] - lr[i]) - step1 * (p1[i] + lp1[i])
            for i in range(own[0] - 1, own[1] + 2)
        }
        lr2 = lap(r2, range(own[0], own[1] + 1))
        s = {i: height(v, i) + (step0 * r[i] + step1 * p1[i]) for i in own}
        parts += [dot(r2, lr2), dot(r2, lp1), dot(p1, lp1)]
        parts += [dot(s, s), dot(s, r2), dot(s, p1), dot(r2, r2), dot(r2, p1), dot(p1, p1)]
        sol.append(s)
        dir1.append(p1)
        res2.append(r2)
        rr1s.append(rr1)
    for a in (sol[0], res2[0], dir1[0]):
        for b in (sol[1], res2[1], dir1[1]):
            parts.append(dot(a, b))
    sums = all_sum(1, parts)
    weights, final = [], []
    for v in range(2):
        r2lr2, r2lp1, p1lp1, ss, sr, sp, rr2, rp, pp = sums[9 * v : 9 * v + 9]
        beta1 = rr2 / rr1s[v]
        p2ap2 = (
            (rr2 + r2lr2) + 2.0 * beta1 * (rp + r2lp1) + beta1 * beta1 * (pp + p1lp1)
        )
        step2 = rr2 / p2ap2
        e, f = step2, step2 * beta1
        weights.append((e, f))
        final.append(
            ss + 2.0 * (e * sr + f * sp) + (e * e * rr2 + 2.0 * e * f * rp + f * f * pp)
        )
        for c in range(2):
            i = own[c]
            sout[v, col(c), :] = sol[v][i] + (e * res2[v][i] + f * dir1[v][i])
    cross_parts = sums[18:]
    (e0, f0), (e1, f1) = weights
    wa, wb = (None, e0, f0), (None, e1, f1)
    mix = cross_parts[0]
    for i in range(3):
        for j in range(3):
            if i == 0 and j == 0:
                continue
            term = cross_parts[3 * i + j]
            if wa[i] is not None:
                term = term * wa[i]
            if wb[j] is not None:
                term = term * wb[j]
            mix = mix + term
    count = float((levels + 1) * 2 * 8 * 128 * n)
    gram_one = (gram_t[0] + final[0]) / count
    gram_mix = (gram_t[1] + mix) / count
    gram_two = (gram_t[2] + final[1]) / count
    scale_one = jnp.sqrt(gram_one + EPSILON)
    cross = gram_mix / scale_one
    rest = gram_two - 2.0 * cross * cross + cross * cross * gram_one / (gram_one + EPSILON)
    scale_two = jnp.sqrt(rest + EPSILON)
    growth = jnp.where(lane == 0, scale_one, jnp.where(lane == 1, cross, scale_two))
    gout[...] = growth

    for g in range(len(chunks)):
        for side in range(2):
            a_copy(g, side).wait_send()
            b_copy(g, side).wait_send()
    for s in shifts:
        halo_copy(stat, st_send, st_recv, s).wait_send()
        halo_copy(ster, se_send, se_recv, s).wait_send()
    for turn in range(2):
        pltpu.make_async_copy(
            red.at[turn, pl.ds(0, n - 1)], red.at[turn, pl.ds(0, n - 1)], rd_send.at[turn]
        ).wait()


def packed(x):
    lead, (cols, rows) = x.shape[:-2], x.shape[-2:]
    x = x.reshape(lead + (cols, rows // 128, 128))
    x = jnp.swapaxes(x, -3, -2)
    return x.reshape(lead + (cols * (rows // 128), 128))


def unpacked(x, cols):
    lead, (rows, lanes) = x.shape[:-2], x.shape[-2:]
    x = x.reshape(lead + (rows // cols, cols, lanes))
    x = jnp.swapaxes(x, -3, -2)
    return x.reshape(lead + (cols, rows // cols * lanes))


def on_device(n, tracer_pert, surface_pert, zonal_flow, merid_flow, bottom_level):
    vectors, levels, columns, rows = tracer_pert.shape
    count = len(chunk_bounds(levels))
    f32 = jnp.float32
    vmem = pl.BlockSpec(memory_space=pltpu.VMEM)
    dma = pltpu.SemaphoreType.DMA
    slots = 2 * REACH + 1
    tracer, surface, tail = pl.pallas_call(
        functools.partial(kernel, n),
        out_shape=(
            jax.ShapeDtypeStruct((vectors, levels, 16, 128), f32),
            jax.ShapeDtypeStruct((vectors, 16, 128), f32),
            jax.ShapeDtypeStruct((8, 128), f32),
        ),
        in_specs=[vmem] * 5,
        out_specs=(vmem,) * 3,
        scratch_shapes=[
            pltpu.VMEM((2, levels, 3, 8, 128), f32),
            pltpu.VMEM((2, levels, 3, 8, 128), f32),
            pltpu.VMEM((2, levels, 2, 8, 128), f32),
            pltpu.VMEM((2, levels, 2, 8, 128), f32),
            pltpu.VMEM((levels, 10, 8, 128), f32),
            pltpu.VMEM((slots, 6, 8, 128), f32),
            pltpu.VMEM((slots, 4, 8, 128), f32),
            pltpu.VMEM((2, 8, 128), f32),
            pltpu.VMEM((2, n, 8, 128), f32),
            dma((2, count)),
            dma((2, count)),
            dma((2, count)),
            dma((2, count)),
            dma((slots,)),
            dma((slots,)),
            dma((slots,)),
            dma((slots,)),
            dma((2,)),
            dma((2,)),
        ],
        compiler_params=pltpu.CompilerParams(
            collective_id=0, has_side_effects=True, vmem_limit_bytes=40 * 1024 * 1024
        ),
    )(
        packed(tracer_pert),
        packed(surface_pert),
        packed(zonal_flow),
        packed(merid_flow),
        packed(bottom_level),
    )
    growth = tail[0, :3]
    scale_one, cross, scale_two = growth[0], growth[1], growth[2]

    def renormalized(x):
        unit = x[0] / scale_one
        rest = (x[1] - cross * unit) / scale_two
        return unpacked(jnp.stack([unit, rest]), columns)

    return renormalized(tracer), renormalized(surface), growth


def solution(mesh):
    placed = (
        P("grp", None, "lon", None),
        P("grp", "lon", None),
        P(None, "lon", None),
        P(None, "lon", None),
        P("lon", None),
    )
    return jax.shard_map(
        functools.partial(on_device, mesh.shape["lon"]),
        mesh=mesh,
        in_specs=placed,
        out_specs=(P("grp", None, "lon", None), P("grp", "lon", None), P("grp")),
        check_vma=False,
    )
```

```python
import functools

import jax
import jax.numpy as jnp
from jax import lax
from jax.experimental import pallas as pl
from jax.experimental.pallas import tpu as pltpu
from jax.sharding import PartitionSpec as P

DIFFUSIVITY = 0.5
TIME_STEP = 0.2
SURFACE_COUPLING = 0.5
STERIC_GAIN = 2.0
EPSILON = 1e-06
MESH = pl.DeviceIdType.MESH
CHUNKS = 5
UNROLL = 2
REACH = 2


def chunk_bounds(levels):
    count = min(CHUNKS, levels)
    edges = [levels * i // count for i in range(count + 1)]
    return list(zip(edges[:-1], edges[1:]))


def peers_loop(n, body):
    if n <= 16:
        for i in range(1, n):
            body(i)
    else:

        def step(i, carry):
            body(i)
            return carry

        lax.fori_loop(1, n, step, 0)


def kernel(
    n, trc_hbm, surf_hbm, zon_hbm, mer_hbm, bot_hbm, out, sout, gout,
    trc, surf, zon, mer, bot, in_sem, few_sem, s_a, r_a, s_b, r_b, coef, stat, ster, pack, red,
    a_send, a_recv, b_send, b_recv, st_send, st_recv, se_send, se_recv, rd_send, rd_recv,
):
    me = lax.axis_index("lon")
    levels = zon_hbm.shape[0]
    chunks = chunk_bounds(levels)
    right, left = lax.rem(me + 1, n), lax.rem(me + n - 1, n)
    side_dev = (left, right)
    tile = (8, 128)
    lane = lax.broadcasted_iota(jnp.int32, tile, 1)
    row = lax.broadcasted_iota(jnp.int32, tile, 0)
    last_lane, first_lane = lane == 127, lane == 0

    def north(x):
        rolled = pltpu.roll(x, 127, 1)
        return jnp.where(last_lane, pltpu.roll(rolled, 7, 0), rolled)

    def south(x):
        rolled = pltpu.roll(x, 1, 1)
        return jnp.where(first_lane, pltpu.roll(rolled, 1, 0), rolled)

    def col(c):
        return pl.ds(c, 8, stride=2)

    def in_copies(g):
        k0, k1 = chunks[g]
        ks = pl.ds(k0, k1 - k0)
        return (
            pltpu.make_async_copy(trc_hbm.at[:, ks], trc.at[:, ks], in_sem.at[g, 0]),
            pltpu.make_async_copy(zon_hbm.at[ks], zon.at[ks], in_sem.at[g, 1]),
        )

    bot_in = pltpu.make_async_copy(bot_hbm, bot, few_sem.at[0])
    surf_in = pltpu.make_async_copy(surf_hbm, surf, few_sem.at[1])
    mer_in = pltpu.make_async_copy(mer_hbm, mer, few_sem.at[2])
    for copy in in_copies(0):
        copy.start()
    bot_in.start()
    surf_in.start()
    for g in range(1, len(chunks)):
        for copy in in_copies(g):
            copy.start()
    mer_in.start()

    barrier = pltpu.get_barrier_semaphore()

    def greet(i):
        pl.semaphore_signal(
            barrier, inc=1, device_id={"lon": lax.rem(me + i, n)}, device_id_type=MESH
        )

    peers_loop(n, greet)

    def gather_chunk(g):
        for copy in in_copies(g):
            copy.wait()
        k0, k1 = chunks[g]

        def step(k, carry):
            for c in range(2):
                s_a[c, k, 0] = trc[0, k, col(c), :]
                s_a[c, k, 1] = trc[1, k, col(c), :]
                s_a[c, k, 2] = zon[k, col(c), :]
            return carry

        lax.fori_loop(k0, k1, step, 0, unroll=UNROLL)

    gather_chunk(0)

    bot_in.wait()
    surf_in.wait()
    for c in range(2):
        d = bot[col(c), :].astype(jnp.float32)
        stat[REACH, 4 + c] = d
        for v in range(2):
            stat[REACH, 2 * v + c] = jnp.where(d > 0, surf[v, col(c), :], 0.0)

    def a_copy(g, side):
        k0, k1 = chunks[g]
        return pltpu.make_async_remote_copy(
            src_ref=s_a.at[side, pl.ds(k0, k1 - k0)],
            dst_ref=r_a.at[1 - side, pl.ds(k0, k1 - k0)],
            send_sem=a_send.at[side, g],
            recv_sem=a_recv.at[1 - side, g],
            device_id={"lon": side_dev[side]},
            device_id_type=MESH,
        )

    def b_copy(g, side):
        k0, k1 = chunks[g]
        return pltpu.make_async_remote_copy(
            src_ref=s_b.at[side, pl.ds(k0, k1 - k0)],
            dst_ref=r_b.at[1 - side, pl.ds(k0, k1 - k0)],
            send_sem=b_send.at[side, g],
            recv_sem=b_recv.at[1 - side, g],
            device_id={"lon": side_dev[side]},
            device_id_type=MESH,
        )

    shifts = [s for s in range(-REACH, REACH + 1) if s != 0]
    shifts.sort(key=abs)

    def halo_copy(buf, send, recv, s):
        return pltpu.make_async_remote_copy(
            src_ref=buf.at[REACH],
            dst_ref=buf.at[REACH - s],
            send_sem=send.at[REACH - s],
            recv_sem=recv.at[REACH - s],
            device_id={"lon": lax.rem(me + s + n, n)},
            device_id_type=MESH,
        )

    pl.semaphore_wait(barrier, n - 1)
    for side in range(2):
        a_copy(0, side).start()
    for s in shifts:
        halo_copy(stat, st_send, st_recv, s).start()
    for g in range(1, len(chunks)):
        gather_chunk(g)
        for side in range(2):
            a_copy(g, side).start()

    for s in shifts:
        halo_copy(stat, st_send, st_recv, s).wait_recv()
    width = 2 * (2 * REACH + 1)
    mid = 2 * REACH

    def depth(i):
        return stat[i // 2, 4 + i % 2]

    def height(v, i):
        return stat[i // 2, 2 * v + i % 2]

    def y_face(i):
        d = depth(i)
        wall = jnp.logical_and(last_lane, row == 7)
        return jnp.where(wall, 0.0, jnp.minimum(d, north(d)))

    def x_face(i):
        return jnp.minimum(depth(i), depth(i + 1))

    half = TIME_STEP * 0.25
    diff = TIME_STEP * DIFFUSIVITY

    mer_in.wait()
    for g, (k0, k1) in enumerate(chunks):
        for side in range(2):
            a_copy(g, side).wait_recv()

        def first(k, carry):
            kf = k.astype(jnp.float32)
            z = (r_a[0, k, 2], s_a[0, k, 2], s_a[1, k, 2], r_a[1, k, 2])
            cx = []
            for f in range(3):
                open_f = kf < x_face(mid - 1 + f)
                u = half * (z[f] + z[f + 1])
                cx.append((jnp.where(open_f, u + diff, 0.0), jnp.where(open_f, u - diff, 0.0)))
            cy = []
            for c in range(2):
                open_f = kf < faces_y[c]
                m = mer[k, col(c), :]
                u = half * (m + north(m))
                cy.append((jnp.where(open_f, u + diff, 0.0), jnp.where(open_f, u - diff, 0.0)))
            for q, (lo, hi) in enumerate(cx + cy):
                coef[k, 2 * q] = lo
                coef[k, 2 * q + 1] = hi
            wet = [kf < depth(mid + c) for c in range(2)]
            for v in range(2):
                t = (
                    r_a[0, k, v],
                    jnp.where(wet[0], s_a[0, k, v], 0.0),
                    jnp.where(wet[1], s_a[1, k, v], 0.0),
                    r_a[1, k, v],
                )
                fx = [cx[f][0] * t[f] + cx[f][1] * t[f + 1] for f in range(3)]
                for c in range(2):
                    fy = cy[c][0] * t[c + 1] + cy[c][1] * north(t[c + 1])
                    s_b[c, k, v] = t[c + 1] - ((fx[c + 1] - fx[c]) + (fy - south(fy)))
            return carry

        if g == 0:
            faces_y = [y_face(mid + c) for c in range(2)]
        lax.fori_loop(k0, k1, first, 0, unroll=UNROLL)
        for side in range(2):
            b_copy(g, side).start()

    face_x = {i: SURFACE_COUPLING * x_face(i) for i in range(0, width - 1)}
    face_y = {i: SURFACE_COUPLING * y_face(i) for i in range(1, width - 1)}

    def lap(s, cols):
        gx = {i: face_x[i] * (s[i + 1] - s[i]) for i in range(cols[0] - 1, cols[-1] + 1)}
        res = {}
        for i in cols:
            gy = face_y[i] * (north(s[i]) - s[i])
            res[i] = -((gx[i] - gx[i - 1]) + (gy - south(gy)))
        return res

    lap_h = [
        lap({i: height(v, i) for i in range(width)}, range(1, width - 1)) for v in range(2)
    ]

    zero = jnp.zeros(tile, jnp.float32)
    totals = (zero,) * 7
    for g, (k0, k1) in enumerate(chunks):
        for side in range(2):
            b_copy(g, side).wait_recv()

        def second(k, carry):
            sums, grams = list(carry[:4]), list(carry[4:])
            cx = [(coef[k, 2 * f], coef[k, 2 * f + 1]) for f in range(3)]
            cy = [(coef[k, 6 + 2 * c], coef[k, 7 + 2 * c]) for c in range(2)]
            new = []
            for v in range(2):
                t = (r_b[0, k, v], s_b[0, k, v], s_b[1, k, v], r_b[1, k, v])
                fx = [cx[f][0] * t[f] + cx[f][1] * t[f + 1] for f in range(3)]
                for c in range(2):
                    fy = cy[c][0] * t[c + 1] + cy[c][1] * north(t[c + 1])
                    val = t[c + 1] - ((fx[c + 1] - fx[c]) + (fy - south(fy)))
                    out[v, k, col(c), :] = val
                    sums[2 * v + c] = sums[2 * v + c] + val
                    new.append(val)
            grams[0] = grams[0] + (new[0] * new[0] + new[1] * new[1])
            grams[1] = grams[1] + (new[0] * new[2] + new[1] * new[3])
            grams[2] = grams[2] + (new[2] * new[2] + new[3] * new[3])
            return tuple(sums + grams)

        totals = lax.fori_loop(k0, k1, second, totals, unroll=UNROLL)

    for q in range(4):
        ster[REACH, q] = totals[q]
    for s in shifts:
        halo_copy(ster, se_send, se_recv, s).start()

    def total_of(x):
        return jnp.sum(jnp.sum(x, axis=1, keepdims=True), axis=0, keepdims=True)

    def red_copy(turn, i):
        return pltpu.make_async_remote_copy(
            src_ref=pack.at[turn],
            dst_ref=red.at[turn, me],
            send_sem=rd_send.at[turn],
            recv_sem=rd_recv.at[turn],
            device_id={"lon": lax.rem(me + i, n)},
            device_id_type=MESH,
        )

    def all_sum(turn, parts):
        mine = zero
        for q, part in enumerate(parts):
            mine = jnp.where(lane == q, total_of(part), mine)
        pack[turn] = mine
        red[turn, me] = mine
        peers_loop(n, lambda i: red_copy(turn, i).start())
        every = pltpu.make_async_copy(
            red.at[turn, pl.ds(0, n - 1)], red.at[turn, pl.ds(0, n - 1)], rd_recv.at[turn]
        )
        every.wait()
        terms = [red[turn, i] for i in range(n)]
        while len(terms) > 1:
            terms = [
                terms[i] + terms[i + 1] if i + 1 < len(terms) else terms[i]
                for i in range(0, len(terms), 2)
            ]
        return [terms[0][0:1, q : q + 1] for q in range(len(parts))]

    gram_parts = list(totals[4:])
    for s in shifts:
        halo_copy(ster, se_send, se_recv, s).wait_recv()

    own = (mid, mid + 1)

    def dot(a, b):
        return a[own[0]] * b[own[0]] + a[own[1]] * b[own[1]]

    gain = STERIC_GAIN / levels
    res, lres, llres, parts = [], [], [], []
    for v in range(2):
        r = {
            i: gain * ster[i // 2, 2 * v + i % 2] - lap_h[v][i] for i in range(1, width - 1)
        }
        lr = lap(r, range(2, width - 2))
        llr = lap(lr, range(own[0], own[1] + 1))
        res.append(r)
        lres.append(lr)
        parts += [dot(r, r), dot(r, lr), dot(lr, lr), dot(lr, llr)]
    sums = all_sum(0, parts + gram_parts)
    gram_t = sums[8:]

    sol, dir1, res2, rr1s, parts = [], [], [], [], []
    ldir1s = []
    for v in range(2):
        l0, l1, l2, l3 = sums[4 * v : 4 * v + 4]
        step0 = l0 / (l0 + l1)
        ratio = l1 / l0
        rr1 = step0 * step0 * jnp.maximum(l2 - l1 * ratio, 0.0)
        beta0 = rr1 / l0
        along = step0 * ratio + beta0
        p1ap1 = (
            along * along * (l0 + l1)
            - 2.0 * along * step0 * (l1 + l2)
            + step0 * step0 * (l2 + l3)
        )
        step1 = rr1 / p1ap1
        r, lr = res[v], lres[v]
        p1 = {i: along * r[i] - step0 * lr[i] for i in range(own[0] - 2, own[1] + 3)}
        lp1 = lap(p1, range(own[0] - 1, own[1] + 2))
        r2 = {
            i: step0 * (ratio * r[i] - lr[i]) - step1 * (p1[i] + lp1[i])
            for i in range(own[0] - 1, own[1] + 2)
        }
        lr2 = lap(r2, range(own[0], own[1] + 1))
        s = {i: height(v, i) + (step0 * r[i] + step1 * p1[i]) for i in own}
        parts += [dot(r2, lr2), dot(r2, lp1), dot(p1, lp1)]
        parts += [dot(s, s), dot(s, r2), dot(s, p1), dot(r2, r2), dot(r2, p1), dot(p1, p1)]
        sol.append(s)
        dir1.append(p1)
        res2.append(r2)
        rr1s.append(rr1)
    for a in (sol[0], res2[0], dir1[0]):
        for b in (sol[1], res2[1], dir1[1]):
            parts.append(dot(a, b))
    sums = all_sum(1, parts)
    weights, final = [], []
    for v in range(2):
        r2lr2, r2lp1, p1lp1, ss, sr, sp, rr2, rp, pp = sums[9 * v : 9 * v + 9]
        beta1 = rr2 / rr1s[v]
        p2ap2 = (
            (rr2 + r2lr2) + 2.0 * beta1 * (rp + r2lp1) + beta1 * beta1 * (pp + p1lp1)
        )
        step2 = rr2 / p2ap2
        e, f = step2, step2 * beta1
        weights.append((e, f))
        final.append(
            ss + 2.0 * (e * sr + f * sp) + (e * e * rr2 + 2.0 * e * f * rp + f * f * pp)
        )
        for c in range(2):
            i = own[c]
            sout[v, col(c), :] = sol[v][i] + (e * res2[v][i] + f * dir1[v][i])
    cross_parts = sums[18:]
    (e0, f0), (e1, f1) = weights
    wa, wb = (None, e0, f0), (None, e1, f1)
    mix = cross_parts[0]
    for i in range(3):
        for j in range(3):
            if i == 0 and j == 0:
                continue
            term = cross_parts[3 * i + j]
            if wa[i] is not None:
                term = term * wa[i]
            if wb[j] is not None:
                term = term * wb[j]
            mix = mix + term
    count = float((levels + 1) * 2 * 8 * 128 * n)
    gram_one = (gram_t[0] + final[0]) / count
    gram_mix = (gram_t[1] + mix) / count
    gram_two = (gram_t[2] + final[1]) / count
    scale_one = jnp.sqrt(gram_one + EPSILON)
    cross = gram_mix / scale_one
    rest = gram_two - 2.0 * cross * cross + cross * cross * gram_one / (gram_one + EPSILON)
    scale_two = jnp.sqrt(rest + EPSILON)
    growth = jnp.where(lane == 0, scale_one, jnp.where(lane == 1, cross, scale_two))
    gout[...] = growth

    for g in range(len(chunks)):
        for side in range(2):
            a_copy(g, side).wait_send()
            b_copy(g, side).wait_send()
    for s in shifts:
        halo_copy(stat, st_send, st_recv, s).wait_send()
        halo_copy(ster, se_send, se_recv, s).wait_send()
    for turn in range(2):
        pltpu.make_async_copy(
            red.at[turn, pl.ds(0, n - 1)], red.at[turn, pl.ds(0, n - 1)], rd_send.at[turn]
        ).wait()


def finish(trc, surf, scales, out, sout, gout, buf, sbuf, gbuf, sem):
    levels = trc.shape[1]
    chunks = chunk_bounds(levels)
    scale_one = scales[0:1, 0:1]
    cross = scales[0:1, 1:2]
    scale_two = scales[0:1, 2:3]
    inv_one, inv_two = 1.0 / scale_one, 1.0 / scale_two

    def pair(first, second):
        unit = first * inv_one
        return unit, (second - cross * unit) * inv_two

    sbuf[0], sbuf[1] = pair(surf[0], surf[1])
    gbuf[...] = scales[0:1, 0:3]
    copies = [
        pltpu.make_async_copy(sbuf, sout, sem.at[0]),
        pltpu.make_async_copy(gbuf, gout, sem.at[1]),
    ]
    for copy in copies:
        copy.start()
    for g, (k0, k1) in enumerate(chunks):

        def step(k, carry):
            buf[0, k], buf[1, k] = pair(trc[0, k], trc[1, k])
            return carry

        lax.fori_loop(k0, k1, step, 0, unroll=UNROLL)
        ks = pl.ds(k0, k1 - k0)
        copy = pltpu.make_async_copy(buf.at[:, ks], out.at[:, ks], sem.at[2 + g])
        copy.start()
        copies.append(copy)
    for copy in copies:
        copy.wait()


def packed(x):
    lead, (cols, rows) = x.shape[:-2], x.shape[-2:]
    x = x.reshape(lead + (cols, rows // 128, 128))
    x = jnp.swapaxes(x, -3, -2)
    return x.reshape(lead + (cols * (rows // 128), 128))


def unpacked(x, cols):
    lead, (rows, lanes) = x.shape[:-2], x.shape[-2:]
    x = x.reshape(lead + (rows // cols, cols, lanes))
    x = jnp.swapaxes(x, -3, -2)
    return x.reshape(lead + (cols, rows // cols * lanes))


def on_device(n, tracer_pert, surface_pert, zonal_flow, merid_flow, bottom_level):
    vectors, levels, columns, rows = tracer_pert.shape
    count = len(chunk_bounds(levels))
    f32 = jnp.float32
    vmem = pl.BlockSpec(memory_space=pltpu.VMEM)
    dma = pltpu.SemaphoreType.DMA
    slots = 2 * REACH + 1
    tracer, surface, tail = pl.pallas_call(
        functools.partial(kernel, n),
        out_shape=(
            jax.ShapeDtypeStruct((vectors, levels, 16, 128), f32),
            jax.ShapeDtypeStruct((vectors, 16, 128), f32),
            jax.ShapeDtypeStruct((8, 128), f32),
        ),
        in_specs=[pl.BlockSpec(memory_space=pltpu.HBM)] * 5,
        out_specs=(vmem,) * 3,
        scratch_shapes=[
            pltpu.VMEM((vectors, levels, 16, 128), f32),
            pltpu.VMEM((vectors, 16, 128), f32),
            pltpu.VMEM((levels, 16, 128), f32),
            pltpu.VMEM((levels, 16, 128), f32),
            pltpu.VMEM((16, 128), jnp.int32),
            dma((count, 2)),
            dma((3,)),
            pltpu.VMEM((2, levels, 3, 8, 128), f32),
            pltpu.VMEM((2, levels, 3, 8, 128), f32),
            pltpu.VMEM((2, levels, 2, 8, 128), f32),
            pltpu.VMEM((2, levels, 2, 8, 128), f32),
            pltpu.VMEM((levels, 10, 8, 128), f32),
            pltpu.VMEM((slots, 6, 8, 128), f32),
            pltpu.VMEM((slots, 4, 8, 128), f32),
            pltpu.VMEM((2, 8, 128), f32),
            pltpu.VMEM((2, n, 8, 128), f32),
            dma((2, count)),
            dma((2, count)),
            dma((2, count)),
            dma((2, count)),
            dma((slots,)),
            dma((slots,)),
            dma((slots,)),
            dma((slots,)),
            dma((2,)),
            dma((2,)),
        ],
        compiler_params=pltpu.CompilerParams(
            collective_id=0, has_side_effects=True, vmem_limit_bytes=67043328
        ),
    )(
        packed(tracer_pert),
        packed(surface_pert),
        packed(zonal_flow),
        packed(merid_flow),
        packed(bottom_level),
    )
    hbm = pl.BlockSpec(memory_space=pltpu.HBM)
    tracer_vec, surface_vec, growth = pl.pallas_call(
        finish,
        out_shape=(
            jax.ShapeDtypeStruct((vectors, levels, 16, 128), f32),
            jax.ShapeDtypeStruct((vectors, 16, 128), f32),
            jax.ShapeDtypeStruct((1, 3), f32),
        ),
        in_specs=[vmem] * 3,
        out_specs=(hbm,) * 3,
        scratch_shapes=[
            pltpu.VMEM((vectors, levels, 16, 128), f32),
            pltpu.VMEM((vectors, 16, 128), f32),
            pltpu.VMEM((1, 3), f32),
            dma((2 + count,)),
        ],
        compiler_params=pltpu.CompilerParams(vmem_limit_bytes=8 * 1024 * 1024),
    )(tracer, surface, tail)
    return unpacked(tracer_vec, columns), unpacked(surface_vec, columns), growth.reshape(3)


def solution(mesh):
    placed = (
        P("grp", None, "lon", None),
        P("grp", "lon", None),
        P(None, "lon", None),
        P(None, "lon", None),
        P("lon", None),
    )
    return jax.shard_map(
        functools.partial(on_device, mesh.shape["lon"]),
        mesh=mesh,
        in_specs=placed,
        out_specs=(P("grp", None, "lon", None), P("grp", "lon", None), P("grp")),
        check_vma=False,
    )
```

```python
import functools

import jax
import jax.numpy as jnp
from jax import lax
from jax.experimental import pallas as pl
from jax.experimental.pallas import tpu as pltpu
from jax.sharding import PartitionSpec as P

DIFFUSIVITY = 0.5
TIME_STEP = 0.2
SURFACE_COUPLING = 0.5
STERIC_GAIN = 2.0
EPSILON = 1e-06
MESH = pl.DeviceIdType.MESH
CHUNKS = 4
UNROLL = 5
REACH = 2


def chunk_bounds(levels):
    count = min(CHUNKS, levels)
    edges = [levels * i // count for i in range(count + 1)]
    return list(zip(edges[:-1], edges[1:]))


def peers_loop(n, body):
    if n <= 16:
        for i in range(1, n):
            body(i)
    else:

        def step(i, carry):
            body(i)
            return carry

        lax.fori_loop(1, n, step, 0)


def kernel(
    n, trc_hbm, surf_hbm, zon_hbm, mer_hbm, bot_hbm, out_hbm, sout, gout,
    out, out_sem, trc, surf, zon, mer, bot, in_sem, few_sem, s_a, r_a, s_b, r_b, coef, stat, ster, pack, red,
    a_send, a_recv, b_send, b_recv, st_send, st_recv, se_send, se_recv, rd_send, rd_recv,
):
    me = lax.axis_index("lon")
    levels = zon_hbm.shape[0]
    chunks = chunk_bounds(levels)
    right, left = lax.rem(me + 1, n), lax.rem(me + n - 1, n)
    side_dev = (left, right)
    tile = (8, 128)
    lane = lax.broadcasted_iota(jnp.int32, tile, 1)
    row = lax.broadcasted_iota(jnp.int32, tile, 0)
    last_lane, first_lane = lane == 127, lane == 0

    def north(x):
        rolled = pltpu.roll(x, 127, 1)
        return jnp.where(last_lane, pltpu.roll(rolled, 7, 0), rolled)

    def south(x):
        rolled = pltpu.roll(x, 1, 1)
        return jnp.where(first_lane, pltpu.roll(rolled, 1, 0), rolled)

    def col(c):
        return pl.ds(c, 8, stride=2)

    def in_copies(g):
        k0, k1 = chunks[g]
        ks = pl.ds(k0, k1 - k0)
        return (
            pltpu.make_async_copy(trc_hbm.at[:, ks], trc.at[:, ks], in_sem.at[g, 0]),
            pltpu.make_async_copy(zon_hbm.at[ks], zon.at[ks], in_sem.at[g, 1]),
        )

    def out_copy(g):
        k0, k1 = chunks[g]
        ks = pl.ds(k0, k1 - k0)
        return pltpu.make_async_copy(out.at[:, ks], out_hbm.at[:, ks], out_sem.at[g])

    bot_in = pltpu.make_async_copy(bot_hbm, bot, few_sem.at[0])
    surf_in = pltpu.make_async_copy(surf_hbm, surf, few_sem.at[1])
    mer_in = pltpu.make_async_copy(mer_hbm, mer, few_sem.at[2])
    for copy in in_copies(0):
        copy.start()
    bot_in.start()
    surf_in.start()
    for g in range(1, len(chunks)):
        for copy in in_copies(g):
            copy.start()
    mer_in.start()

    barrier = pltpu.get_barrier_semaphore()

    def greet(i):
        pl.semaphore_signal(
            barrier, inc=1, device_id={"lon": lax.rem(me + i, n)}, device_id_type=MESH
        )

    peers_loop(n, greet)

    def gather_chunk(g):
        for copy in in_copies(g):
            copy.wait()
        k0, k1 = chunks[g]

        def step(k, carry):
            for c in range(2):
                s_a[c, k, 0] = trc[0, k, col(c), :]
                s_a[c, k, 1] = trc[1, k, col(c), :]
                s_a[c, k, 2] = zon[k, col(c), :]
            return carry

        lax.fori_loop(k0, k1, step, 0, unroll=UNROLL)

    gather_chunk(0)

    bot_in.wait()
    surf_in.wait()
    for c in range(2):
        d = bot[col(c), :].astype(jnp.float32)
        stat[REACH, 4 + c] = d
        for v in range(2):
            stat[REACH, 2 * v + c] = jnp.where(d > 0, surf[v, col(c), :], 0.0)

    def a_copy(g, side):
        k0, k1 = chunks[g]
        return pltpu.make_async_remote_copy(
            src_ref=s_a.at[side, pl.ds(k0, k1 - k0)],
            dst_ref=r_a.at[1 - side, pl.ds(k0, k1 - k0)],
            send_sem=a_send.at[side, g],
            recv_sem=a_recv.at[1 - side, g],
            device_id={"lon": side_dev[side]},
            device_id_type=MESH,
        )

    def b_copy(g, side):
        k0, k1 = chunks[g]
        return pltpu.make_async_remote_copy(
            src_ref=s_b.at[side, pl.ds(k0, k1 - k0)],
            dst_ref=r_b.at[1 - side, pl.ds(k0, k1 - k0)],
            send_sem=b_send.at[side, g],
            recv_sem=b_recv.at[1 - side, g],
            device_id={"lon": side_dev[side]},
            device_id_type=MESH,
        )

    shifts = [s for s in range(-REACH, REACH + 1) if s != 0]
    shifts.sort(key=abs)

    def halo_copy(buf, send, recv, s):
        return pltpu.make_async_remote_copy(
            src_ref=buf.at[REACH],
            dst_ref=buf.at[REACH - s],
            send_sem=send.at[REACH - s],
            recv_sem=recv.at[REACH - s],
            device_id={"lon": lax.rem(me + s + n, n)},
            device_id_type=MESH,
        )

    pl.semaphore_wait(barrier, n - 1)
    for side in range(2):
        a_copy(0, side).start()
    for s in shifts:
        halo_copy(stat, st_send, st_recv, s).start()
    for g in range(1, len(chunks)):
        gather_chunk(g)
        for side in range(2):
            a_copy(g, side).start()

    for s in shifts:
        halo_copy(stat, st_send, st_recv, s).wait_recv()
    width = 2 * (2 * REACH + 1)
    mid = 2 * REACH

    def depth(i):
        return stat[i // 2, 4 + i % 2]

    def height(v, i):
        return stat[i // 2, 2 * v + i % 2]

    def y_face(i):
        d = depth(i)
        wall = jnp.logical_and(last_lane, row == 7)
        return jnp.where(wall, 0.0, jnp.minimum(d, north(d)))

    def x_face(i):
        return jnp.minimum(depth(i), depth(i + 1))

    half = TIME_STEP * 0.25
    diff = TIME_STEP * DIFFUSIVITY

    mer_in.wait()
    for g, (k0, k1) in enumerate(chunks):
        for side in range(2):
            a_copy(g, side).wait_recv()

        def first(k, carry):
            kf = k.astype(jnp.float32)
            z = (r_a[0, k, 2], s_a[0, k, 2], s_a[1, k, 2], r_a[1, k, 2])
            cx = []
            for f in range(3):
                open_f = kf < x_face(mid - 1 + f)
                u = half * (z[f] + z[f + 1])
                cx.append((jnp.where(open_f, u + diff, 0.0), jnp.where(open_f, u - diff, 0.0)))
            cy = []
            for c in range(2):
                open_f = kf < faces_y[c]
                m = mer[k, col(c), :]
                u = half * (m + north(m))
                cy.append((jnp.where(open_f, u + diff, 0.0), jnp.where(open_f, u - diff, 0.0)))
            for q, (lo, hi) in enumerate(cx + cy):
                coef[k, 2 * q] = lo
                coef[k, 2 * q + 1] = hi
            wet = [kf < depth(mid + c) for c in range(2)]
            for v in range(2):
                t = (
                    r_a[0, k, v],
                    jnp.where(wet[0], s_a[0, k, v], 0.0),
                    jnp.where(wet[1], s_a[1, k, v], 0.0),
                    r_a[1, k, v],
                )
                fx = [cx[f][0] * t[f] + cx[f][1] * t[f + 1] for f in range(3)]
                for c in range(2):
                    fy = cy[c][0] * t[c + 1] + cy[c][1] * north(t[c + 1])
                    s_b[c, k, v] = t[c + 1] - ((fx[c + 1] - fx[c]) + (fy - south(fy)))
            return carry

        if g == 0:
            faces_y = [y_face(mid + c) for c in range(2)]
        lax.fori_loop(k0, k1, first, 0, unroll=UNROLL)
        for side in range(2):
            b_copy(g, side).start()

    face_x = {i: SURFACE_COUPLING * x_face(i) for i in range(0, width - 1)}
    face_y = {i: SURFACE_COUPLING * y_face(i) for i in range(1, width - 1)}

    def lap(s, cols):
        gx = {i: face_x[i] * (s[i + 1] - s[i]) for i in range(cols[0] - 1, cols[-1] + 1)}
        res = {}
        for i in cols:
            gy = face_y[i] * (north(s[i]) - s[i])
            res[i] = -((gx[i] - gx[i - 1]) + (gy - south(gy)))
        return res

    lap_h = [
        lap({i: height(v, i) for i in range(width)}, range(1, width - 1)) for v in range(2)
    ]

    zero = jnp.zeros(tile, jnp.float32)
    totals = (zero,) * 7
    for g, (k0, k1) in enumerate(chunks):
        for side in range(2):
            b_copy(g, side).wait_recv()

        def second(k, carry):
            sums, grams = list(carry[:4]), list(carry[4:])
            cx = [(coef[k, 2 * f], coef[k, 2 * f + 1]) for f in range(3)]
            cy = [(coef[k, 6 + 2 * c], coef[k, 7 + 2 * c]) for c in range(2)]
            new = []
            for v in range(2):
                t = (r_b[0, k, v], s_b[0, k, v], s_b[1, k, v], r_b[1, k, v])
                fx = [cx[f][0] * t[f] + cx[f][1] * t[f + 1] for f in range(3)]
                for c in range(2):
                    fy = cy[c][0] * t[c + 1] + cy[c][1] * north(t[c + 1])
                    val = t[c + 1] - ((fx[c + 1] - fx[c]) + (fy - south(fy)))
                    out[v, k, col(c), :] = val
                    sums[2 * v + c] = sums[2 * v + c] + val
                    new.append(val)
            grams[0] = grams[0] + (new[0] * new[0] + new[1] * new[1])
            grams[1] = grams[1] + (new[0] * new[2] + new[1] * new[3])
            grams[2] = grams[2] + (new[2] * new[2] + new[3] * new[3])
            return tuple(sums + grams)

        totals = lax.fori_loop(k0, k1, second, totals, unroll=UNROLL)
        out_copy(g).start()

    for q in range(4):
        ster[REACH, q] = totals[q]
    for s in shifts:
        halo_copy(ster, se_send, se_recv, s).start()

    def total_of(x):
        return jnp.sum(jnp.sum(x, axis=1, keepdims=True), axis=0, keepdims=True)

    def red_copy(turn, i):
        return pltpu.make_async_remote_copy(
            src_ref=pack.at[turn],
            dst_ref=red.at[turn, me],
            send_sem=rd_send.at[turn],
            recv_sem=rd_recv.at[turn],
            device_id={"lon": lax.rem(me + i, n)},
            device_id_type=MESH,
        )

    def all_sum(turn, parts):
        mine = zero
        for q, part in enumerate(parts):
            mine = jnp.where(lane == q, total_of(part), mine)
        pack[turn] = mine
        red[turn, me] = mine
        peers_loop(n, lambda i: red_copy(turn, i).start())
        every = pltpu.make_async_copy(
            red.at[turn, pl.ds(0, n - 1)], red.at[turn, pl.ds(0, n - 1)], rd_recv.at[turn]
        )
        every.wait()
        terms = [red[turn, i] for i in range(n)]
        while len(terms) > 1:
            terms = [
                terms[i] + terms[i + 1] if i + 1 < len(terms) else terms[i]
                for i in range(0, len(terms), 2)
            ]
        return [terms[0][0:1, q : q + 1] for q in range(len(parts))]

    gram_parts = list(totals[4:])
    for s in shifts:
        halo_copy(ster, se_send, se_recv, s).wait_recv()

    own = (mid, mid + 1)

    def dot(a, b):
        return a[own[0]] * b[own[0]] + a[own[1]] * b[own[1]]

    gain = STERIC_GAIN / levels
    res, lres, llres, parts = [], [], [], []
    for v in range(2):
        r = {
            i: gain * ster[i // 2, 2 * v + i % 2] - lap_h[v][i] for i in range(1, width - 1)
        }
        lr = lap(r, range(2, width - 2))
        llr = lap(lr, range(own[0], own[1] + 1))
        res.append(r)
        lres.append(lr)
        parts += [dot(r, r), dot(r, lr), dot(lr, lr), dot(lr, llr)]
    sums = all_sum(0, parts + gram_parts)
    gram_t = sums[8:]

    sol, dir1, res2, rr1s, parts = [], [], [], [], []
    ldir1s = []
    for v in range(2):
        l0, l1, l2, l3 = sums[4 * v : 4 * v + 4]
        step0 = l0 / (l0 + l1)
        ratio = l1 / l0
        rr1 = step0 * step0 * jnp.maximum(l2 - l1 * ratio, 0.0)
        beta0 = rr1 / l0
        along = step0 * ratio + beta0
        p1ap1 = (
            along * along * (l0 + l1)
            - 2.0 * along * step0 * (l1 + l2)
            + step0 * step0 * (l2 + l3)
        )
        step1 = rr1 / p1ap1
        r, lr = res[v], lres[v]
        p1 = {i: along * r[i] - step0 * lr[i] for i in range(own[0] - 2, own[1] + 3)}
        lp1 = lap(p1, range(own[0] - 1, own[1] + 2))
        r2 = {
            i: step0 * (ratio * r[i] - lr[i]) - step1 * (p1[i] + lp1[i])
            for i in range(own[0] - 1, own[1] + 2)
        }
        lr2 = lap(r2, range(own[0], own[1] + 1))
        s = {i: height(v, i) + (step0 * r[i] + step1 * p1[i]) for i in own}
        parts += [dot(r2, lr2), dot(r2, lp1), dot(p1, lp1)]
        parts += [dot(s, s), dot(s, r2), dot(s, p1), dot(r2, r2), dot(r2, p1), dot(p1, p1)]
        sol.append(s)
        dir1.append(p1)
        res2.append(r2)
        rr1s.append(rr1)
    for a in (sol[0], res2[0], dir1[0]):
        for b in (sol[1], res2[1], dir1[1]):
            parts.append(dot(a, b))
    sums = all_sum(1, parts)
    weights, final = [], []
    for v in range(2):
        r2lr2, r2lp1, p1lp1, ss, sr, sp, rr2, rp, pp = sums[9 * v : 9 * v + 9]
        beta1 = rr2 / rr1s[v]
        p2ap2 = (
            (rr2 + r2lr2) + 2.0 * beta1 * (rp + r2lp1) + beta1 * beta1 * (pp + p1lp1)
        )
        step2 = rr2 / p2ap2
        e, f = step2, step2 * beta1
        weights.append((e, f))
        final.append(
            ss + 2.0 * (e * sr + f * sp) + (e * e * rr2 + 2.0 * e * f * rp + f * f * pp)
        )
        for c in range(2):
            i = own[c]
            sout[v, col(c), :] = sol[v][i] + (e * res2[v][i] + f * dir1[v][i])
    cross_parts = sums[18:]
    (e0, f0), (e1, f1) = weights
    wa, wb = (None, e0, f0), (None, e1, f1)
    mix = cross_parts[0]
    for i in range(3):
        for j in range(3):
            if i == 0 and j == 0:
                continue
            term = cross_parts[3 * i + j]
            if wa[i] is not None:
                term = term * wa[i]
            if wb[j] is not None:
                term = term * wb[j]
            mix = mix + term
    count = float((levels + 1) * 2 * 8 * 128 * n)
    gram_one = (gram_t[0] + final[0]) / count
    gram_mix = (gram_t[1] + mix) / count
    gram_two = (gram_t[2] + final[1]) / count
    scale_one = jnp.sqrt(gram_one + EPSILON)
    cross = gram_mix / scale_one
    rest = gram_two - 2.0 * cross * cross + cross * cross * gram_one / (gram_one + EPSILON)
    scale_two = jnp.sqrt(rest + EPSILON)
    growth = jnp.where(lane == 0, scale_one, jnp.where(lane == 1, cross, scale_two))
    gout[...] = growth

    for g in range(len(chunks)):
        out_copy(g).wait()
        for side in range(2):
            a_copy(g, side).wait_send()
            b_copy(g, side).wait_send()
    for s in shifts:
        halo_copy(stat, st_send, st_recv, s).wait_send()
        halo_copy(ster, se_send, se_recv, s).wait_send()
    for turn in range(2):
        pltpu.make_async_copy(
            red.at[turn, pl.ds(0, n - 1)], red.at[turn, pl.ds(0, n - 1)], rd_send.at[turn]
        ).wait()


def finish(
    trc_hbm, surf_hbm, scales_hbm, out, sout, gout,
    trc, surf, scales, in_sem, buf, sbuf, gbuf, sem,
):
    levels = trc.shape[1]
    chunks = chunk_bounds(levels)
    scales_in = pltpu.make_async_copy(scales_hbm, scales, in_sem.at[0])
    surf_in = pltpu.make_async_copy(surf_hbm, surf, in_sem.at[1])
    scales_in.start()
    surf_in.start()
    ins = []
    for g, (k0, k1) in enumerate(chunks):
        ks = pl.ds(k0, k1 - k0)
        ins.append(pltpu.make_async_copy(trc_hbm.at[:, ks], trc.at[:, ks], in_sem.at[2 + g]))
        ins[-1].start()
    scales_in.wait()
    surf_in.wait()
    scale_one = scales[0:1, 0:1]
    cross = scales[0:1, 1:2]
    scale_two = scales[0:1, 2:3]
    inv_one, inv_two = 1.0 / scale_one, 1.0 / scale_two

    def pair(first, second):
        unit = first * inv_one
        return unit, (second - cross * unit) * inv_two

    sbuf[0], sbuf[1] = pair(surf[0], surf[1])
    gbuf[...] = scales[0:1, 0:3]
    copies = [
        pltpu.make_async_copy(sbuf, sout, sem.at[0]),
        pltpu.make_async_copy(gbuf, gout, sem.at[1]),
    ]
    for copy in copies:
        copy.start()
    for g, (k0, k1) in enumerate(chunks):

        def step(k, carry):
            buf[0, k], buf[1, k] = pair(trc[0, k], trc[1, k])
            return carry

        ins[g].wait()
        lax.fori_loop(k0, k1, step, 0, unroll=UNROLL)
        ks = pl.ds(k0, k1 - k0)
        copy = pltpu.make_async_copy(buf.at[:, ks], out.at[:, ks], sem.at[2 + g])
        copy.start()
        copies.append(copy)
    for copy in copies:
        copy.wait()


def packed(x):
    lead, (cols, rows) = x.shape[:-2], x.shape[-2:]
    x = x.reshape(lead + (cols, rows // 128, 128))
    x = jnp.swapaxes(x, -3, -2)
    return x.reshape(lead + (cols * (rows // 128), 128))


def unpacked(x, cols):
    lead, (rows, lanes) = x.shape[:-2], x.shape[-2:]
    x = x.reshape(lead + (rows // cols, cols, lanes))
    x = jnp.swapaxes(x, -3, -2)
    return x.reshape(lead + (cols, rows // cols * lanes))


def on_device(n, tracer_pert, surface_pert, zonal_flow, merid_flow, bottom_level):
    vectors, levels, columns, rows = tracer_pert.shape
    count = len(chunk_bounds(levels))
    f32 = jnp.float32
    vmem = pl.BlockSpec(memory_space=pltpu.VMEM)
    dma = pltpu.SemaphoreType.DMA
    slots = 2 * REACH + 1
    tracer, surface, tail = pl.pallas_call(
        functools.partial(kernel, n),
        out_shape=(
            jax.ShapeDtypeStruct((vectors, levels, 16, 128), f32),
            jax.ShapeDtypeStruct((vectors, 16, 128), f32),
            jax.ShapeDtypeStruct((8, 128), f32),
        ),
        in_specs=[pl.BlockSpec(memory_space=pltpu.HBM)] * 5,
        out_specs=(pl.BlockSpec(memory_space=pltpu.HBM), vmem, vmem),
        scratch_shapes=[
            pltpu.VMEM((vectors, levels, 16, 128), f32),
            dma((count,)),
            pltpu.VMEM((vectors, levels, 16, 128), f32),
            pltpu.VMEM((vectors, 16, 128), f32),
            pltpu.VMEM((levels, 16, 128), f32),
            pltpu.VMEM((levels, 16, 128), f32),
            pltpu.VMEM((16, 128), jnp.int32),
            dma((count, 2)),
            dma((3,)),
            pltpu.VMEM((2, levels, 3, 8, 128), f32),
            pltpu.VMEM((2, levels, 3, 8, 128), f32),
            pltpu.VMEM((2, levels, 2, 8, 128), f32),
            pltpu.VMEM((2, levels, 2, 8, 128), f32),
            pltpu.VMEM((levels, 10, 8, 128), f32),
            pltpu.VMEM((slots, 6, 8, 128), f32),
            pltpu.VMEM((slots, 4, 8, 128), f32),
            pltpu.VMEM((2, 8, 128), f32),
            pltpu.VMEM((2, n, 8, 128), f32),
            dma((2, count)),
            dma((2, count)),
            dma((2, count)),
            dma((2, count)),
            dma((slots,)),
            dma((slots,)),
            dma((slots,)),
            dma((slots,)),
            dma((2,)),
            dma((2,)),
        ],
        compiler_params=pltpu.CompilerParams(
            collective_id=0, has_side_effects=True, vmem_limit_bytes=67043328
        ),
    )(
        packed(tracer_pert),
        packed(surface_pert),
        packed(zonal_flow),
        packed(merid_flow),
        packed(bottom_level),
    )
    hbm = pl.BlockSpec(memory_space=pltpu.HBM)
    tracer_vec, surface_vec, growth = pl.pallas_call(
        finish,
        out_shape=(
            jax.ShapeDtypeStruct((vectors, levels, 16, 128), f32),
            jax.ShapeDtypeStruct((vectors, 16, 128), f32),
            jax.ShapeDtypeStruct((1, 3), f32),
        ),
        in_specs=[hbm] * 3,
        out_specs=(hbm,) * 3,
        scratch_shapes=[
            pltpu.VMEM((vectors, levels, 16, 128), f32),
            pltpu.VMEM((vectors, 16, 128), f32),
            pltpu.VMEM((8, 128), f32),
            dma((2 + count,)),
            pltpu.VMEM((vectors, levels, 16, 128), f32),
            pltpu.VMEM((vectors, 16, 128), f32),
            pltpu.VMEM((1, 3), f32),
            dma((2 + count,)),
        ],
        compiler_params=pltpu.CompilerParams(vmem_limit_bytes=67043328),
    )(tracer, surface, tail)
    return unpacked(tracer_vec, columns), unpacked(surface_vec, columns), growth.reshape(3)


def solution(mesh):
    placed = (
        P("grp", None, "lon", None),
        P("grp", "lon", None),
        P(None, "lon", None),
        P(None, "lon", None),
        P("lon", None),
    )
    return jax.shard_map(
        functools.partial(on_device, mesh.shape["lon"]),
        mesh=mesh,
        in_specs=placed,
        out_specs=(P("grp", None, "lon", None), P("grp", "lon", None), P("grp")),
        check_vma=False,
    )
```

```python
import functools

import jax
import jax.numpy as jnp
from jax import lax
from jax.experimental import pallas as pl
from jax.experimental.pallas import tpu as pltpu
from jax.sharding import PartitionSpec as P

DIFFUSIVITY = 0.5
TIME_STEP = 0.2
SURFACE_COUPLING = 0.5
STERIC_GAIN = 2.0
EPSILON = 1e-06
MESH = pl.DeviceIdType.MESH
CHUNK_EDGES = (0, 34, 64, 88, 100)
UNROLL = 5
REACH = 2


def chunk_bounds(levels):
    edges = sorted({levels * part // 100 for part in CHUNK_EDGES})
    return list(zip(edges[:-1], edges[1:]))


def peers_loop(n, body):
    if n <= 16:
        for i in range(1, n):
            body(i)
    else:

        def step(i, carry):
            body(i)
            return carry

        lax.fori_loop(1, n, step, 0)


def kernel(
    n, trc_hbm, surf_hbm, zon_hbm, mer_hbm, bot_hbm, out_hbm, sout, gout,
    out, out_sem, trc, surf, zon, mer, bot, in_sem, few_sem, s_a, r_a, s_b, r_b, coef, stat, ster, pack, red,
    a_send, a_recv, b_send, b_recv, st_send, st_recv, se_send, se_recv, rd_send, rd_recv,
):
    me = lax.axis_index("lon")
    levels = zon_hbm.shape[0]
    chunks = chunk_bounds(levels)
    right, left = lax.rem(me + 1, n), lax.rem(me + n - 1, n)
    side_dev = (left, right)
    tile = (8, 128)
    lane = lax.broadcasted_iota(jnp.int32, tile, 1)
    row = lax.broadcasted_iota(jnp.int32, tile, 0)
    last_lane, first_lane = lane == 127, lane == 0

    def north(x):
        rolled = pltpu.roll(x, 127, 1)
        return jnp.where(last_lane, pltpu.roll(rolled, 7, 0), rolled)

    def south(x):
        rolled = pltpu.roll(x, 1, 1)
        return jnp.where(first_lane, pltpu.roll(rolled, 1, 0), rolled)

    def col(c):
        return pl.ds(c, 8, stride=2)

    def in_copies(g):
        k0, k1 = chunks[g]
        ks = pl.ds(k0, k1 - k0)
        return (
            pltpu.make_async_copy(trc_hbm.at[:, ks], trc.at[:, ks], in_sem.at[g, 0]),
            pltpu.make_async_copy(zon_hbm.at[ks], zon.at[ks], in_sem.at[g, 1]),
        )

    def out_copy(g):
        k0, k1 = chunks[g]
        ks = pl.ds(k0, k1 - k0)
        return pltpu.make_async_copy(out.at[:, ks], out_hbm.at[:, ks], out_sem.at[g])

    bot_in = pltpu.make_async_copy(bot_hbm, bot, few_sem.at[0])
    surf_in = pltpu.make_async_copy(surf_hbm, surf, few_sem.at[1])
    mer_in = pltpu.make_async_copy(mer_hbm, mer, few_sem.at[2])
    for copy in in_copies(0):
        copy.start()
    bot_in.start()
    surf_in.start()
    for g in range(1, len(chunks)):
        for copy in in_copies(g):
            copy.start()
    mer_in.start()

    barrier = pltpu.get_barrier_semaphore()

    def greet(i):
        pl.semaphore_signal(
            barrier, inc=1, device_id={"lon": lax.rem(me + i, n)}, device_id_type=MESH
        )

    peers_loop(n, greet)

    def gather_chunk(g):
        for copy in in_copies(g):
            copy.wait()
        k0, k1 = chunks[g]

        def step(k, carry):
            for c in range(2):
                s_a[c, k, 0] = trc[0, k, col(c), :]
                s_a[c, k, 1] = trc[1, k, col(c), :]
                s_a[c, k, 2] = zon[k, col(c), :]
            return carry

        lax.fori_loop(k0, k1, step, 0, unroll=UNROLL)

    gather_chunk(0)

    bot_in.wait()
    surf_in.wait()
    for c in range(2):
        d = bot[col(c), :].astype(jnp.float32)
        stat[REACH, 4 + c] = d
        for v in range(2):
            stat[REACH, 2 * v + c] = jnp.where(d > 0, surf[v, col(c), :], 0.0)

    def a_copy(g, side):
        k0, k1 = chunks[g]
        return pltpu.make_async_remote_copy(
            src_ref=s_a.at[side, pl.ds(k0, k1 - k0)],
            dst_ref=r_a.at[1 - side, pl.ds(k0, k1 - k0)],
            send_sem=a_send.at[side, g],
            recv_sem=a_recv.at[1 - side, g],
            device_id={"lon": side_dev[side]},
            device_id_type=MESH,
        )

    def b_copy(g, side):
        k0, k1 = chunks[g]
        return pltpu.make_async_remote_copy(
            src_ref=s_b.at[side, pl.ds(k0, k1 - k0)],
            dst_ref=r_b.at[1 - side, pl.ds(k0, k1 - k0)],
            send_sem=b_send.at[side, g],
            recv_sem=b_recv.at[1 - side, g],
            device_id={"lon": side_dev[side]},
            device_id_type=MESH,
        )

    shifts = [s for s in range(-REACH, REACH + 1) if s != 0]
    shifts.sort(key=abs)

    def halo_copy(buf, send, recv, s):
        return pltpu.make_async_remote_copy(
            src_ref=buf.at[REACH],
            dst_ref=buf.at[REACH - s],
            send_sem=send.at[REACH - s],
            recv_sem=recv.at[REACH - s],
            device_id={"lon": lax.rem(me + s + n, n)},
            device_id_type=MESH,
        )

    pl.semaphore_wait(barrier, n - 1)
    for side in range(2):
        a_copy(0, side).start()
    for s in shifts:
        halo_copy(stat, st_send, st_recv, s).start()
    for g in range(1, len(chunks)):
        gather_chunk(g)
        for side in range(2):
            a_copy(g, side).start()

    for s in shifts[:2]:
        halo_copy(stat, st_send, st_recv, s).wait_recv()
    width = 2 * (2 * REACH + 1)
    mid = 2 * REACH

    def depth(i):
        return stat[i // 2, 4 + i % 2]

    def height(v, i):
        return stat[i // 2, 2 * v + i % 2]

    def y_face(i):
        d = depth(i)
        wall = jnp.logical_and(last_lane, row == 7)
        return jnp.where(wall, 0.0, jnp.minimum(d, north(d)))

    def x_face(i):
        return jnp.minimum(depth(i), depth(i + 1))

    half = TIME_STEP * 0.25
    diff = TIME_STEP * DIFFUSIVITY

    mer_in.wait()
    for g, (k0, k1) in enumerate(chunks):
        for side in range(2):
            a_copy(g, side).wait_recv()

        def first(k, carry):
            kf = k.astype(jnp.float32)
            z = (r_a[0, k, 2], s_a[0, k, 2], s_a[1, k, 2], r_a[1, k, 2])
            cx = []
            for f in range(3):
                open_f = kf < x_face(mid - 1 + f)
                u = half * (z[f] + z[f + 1])
                cx.append((jnp.where(open_f, u + diff, 0.0), jnp.where(open_f, u - diff, 0.0)))
            cy = []
            for c in range(2):
                open_f = kf < faces_y[c]
                m = mer[k, col(c), :]
                u = half * (m + north(m))
                cy.append((jnp.where(open_f, u + diff, 0.0), jnp.where(open_f, u - diff, 0.0)))
            for q, (lo, hi) in enumerate(cx + cy):
                coef[k, 2 * q] = lo
                coef[k, 2 * q + 1] = hi
            wet = [kf < depth(mid + c) for c in range(2)]
            for v in range(2):
                t = (
                    r_a[0, k, v],
                    jnp.where(wet[0], s_a[0, k, v], 0.0),
                    jnp.where(wet[1], s_a[1, k, v], 0.0),
                    r_a[1, k, v],
                )
                fx = [cx[f][0] * t[f] + cx[f][1] * t[f + 1] for f in range(3)]
                for c in range(2):
                    fy = cy[c][0] * t[c + 1] + cy[c][1] * north(t[c + 1])
                    s_b[c, k, v] = t[c + 1] - ((fx[c + 1] - fx[c]) + (fy - south(fy)))
            return carry

        if g == 0:
            faces_y = [y_face(mid + c) for c in range(2)]
        lax.fori_loop(k0, k1, first, 0, unroll=UNROLL)
        for side in range(2):
            b_copy(g, side).start()

    for s in shifts[2:]:
        halo_copy(stat, st_send, st_recv, s).wait_recv()

    face_x = {i: SURFACE_COUPLING * x_face(i) for i in range(0, width - 1)}
    face_y = {i: SURFACE_COUPLING * y_face(i) for i in range(1, width - 1)}

    def lap(s, cols):
        gx = {i: face_x[i] * (s[i + 1] - s[i]) for i in range(cols[0] - 1, cols[-1] + 1)}
        res = {}
        for i in cols:
            gy = face_y[i] * (north(s[i]) - s[i])
            res[i] = -((gx[i] - gx[i - 1]) + (gy - south(gy)))
        return res

    lap_h = [
        lap({i: height(v, i) for i in range(width)}, range(1, width - 1)) for v in range(2)
    ]

    zero = jnp.zeros(tile, jnp.float32)
    totals = (zero,) * 7
    for g, (k0, k1) in enumerate(chunks):
        for side in range(2):
            b_copy(g, side).wait_recv()

        def second(k, carry):
            sums, grams = list(carry[:4]), list(carry[4:])
            cx = [(coef[k, 2 * f], coef[k, 2 * f + 1]) for f in range(3)]
            cy = [(coef[k, 6 + 2 * c], coef[k, 7 + 2 * c]) for c in range(2)]
            new = []
            for v in range(2):
                t = (r_b[0, k, v], s_b[0, k, v], s_b[1, k, v], r_b[1, k, v])
                fx = [cx[f][0] * t[f] + cx[f][1] * t[f + 1] for f in range(3)]
                for c in range(2):
                    fy = cy[c][0] * t[c + 1] + cy[c][1] * north(t[c + 1])
                    val = t[c + 1] - ((fx[c + 1] - fx[c]) + (fy - south(fy)))
                    out[v, k, col(c), :] = val
                    sums[2 * v + c] = sums[2 * v + c] + val
                    new.append(val)
            grams[0] = grams[0] + (new[0] * new[0] + new[1] * new[1])
            grams[1] = grams[1] + (new[0] * new[2] + new[1] * new[3])
            grams[2] = grams[2] + (new[2] * new[2] + new[3] * new[3])
            return tuple(sums + grams)

        totals = lax.fori_loop(k0, k1, second, totals, unroll=UNROLL)
        out_copy(g).start()

    for q in range(4):
        ster[REACH, q] = totals[q]
    for s in shifts:
        halo_copy(ster, se_send, se_recv, s).start()

    def total_of(x):
        return jnp.sum(jnp.sum(x, axis=1, keepdims=True), axis=0, keepdims=True)

    def red_copy(turn, i):
        return pltpu.make_async_remote_copy(
            src_ref=pack.at[turn],
            dst_ref=red.at[turn, me],
            send_sem=rd_send.at[turn],
            recv_sem=rd_recv.at[turn],
            device_id={"lon": lax.rem(me + i, n)},
            device_id_type=MESH,
        )

    def all_sum(turn, parts):
        mine = zero
        for q, part in enumerate(parts):
            mine = jnp.where(lane == q, total_of(part), mine)
        pack[turn] = mine[0:1]
        red[turn, me] = mine[0:1]
        peers_loop(n, lambda i: red_copy(turn, i).start())
        every = pltpu.make_async_copy(
            red.at[turn, pl.ds(0, n - 1)], red.at[turn, pl.ds(0, n - 1)], rd_recv.at[turn]
        )
        every.wait()
        terms = [red[turn, i] for i in range(n)]
        while len(terms) > 1:
            terms = [
                terms[i] + terms[i + 1] if i + 1 < len(terms) else terms[i]
                for i in range(0, len(terms), 2)
            ]
        return [terms[0][0:1, q : q + 1] for q in range(len(parts))]

    gram_parts = list(totals[4:])
    for s in shifts:
        halo_copy(ster, se_send, se_recv, s).wait_recv()

    own = (mid, mid + 1)

    def dot(a, b):
        return a[own[0]] * b[own[0]] + a[own[1]] * b[own[1]]

    gain = STERIC_GAIN / levels
    res, lres, llres, parts = [], [], [], []
    for v in range(2):
        r = {
            i: gain * ster[i // 2, 2 * v + i % 2] - lap_h[v][i] for i in range(1, width - 1)
        }
        lr = lap(r, range(2, width - 2))
        llr = lap(lr, range(own[0], own[1] + 1))
        res.append(r)
        lres.append(lr)
        parts += [dot(r, r), dot(r, lr), dot(lr, lr), dot(lr, llr)]
    sums = all_sum(0, parts + gram_parts)
    gram_t = sums[8:]

    sol, dir1, res2, rr1s, parts = [], [], [], [], []
    ldir1s = []
    for v in range(2):
        l0, l1, l2, l3 = sums[4 * v : 4 * v + 4]
        step0 = l0 / (l0 + l1)
        ratio = l1 / l0
        rr1 = step0 * step0 * jnp.maximum(l2 - l1 * ratio, 0.0)
        beta0 = rr1 / l0
        along = step0 * ratio + beta0
        p1ap1 = (
            along * along * (l0 + l1)
            - 2.0 * along * step0 * (l1 + l2)
            + step0 * step0 * (l2 + l3)
        )
        step1 = rr1 / p1ap1
        r, lr = res[v], lres[v]
        p1 = {i: along * r[i] - step0 * lr[i] for i in range(own[0] - 2, own[1] + 3)}
        lp1 = lap(p1, range(own[0] - 1, own[1] + 2))
        r2 = {
            i: step0 * (ratio * r[i] - lr[i]) - step1 * (p1[i] + lp1[i])
            for i in range(own[0] - 1, own[1] + 2)
        }
        lr2 = lap(r2, range(own[0], own[1] + 1))
        s = {i: height(v, i) + (step0 * r[i] + step1 * p1[i]) for i in own}
        parts += [dot(r2, lr2), dot(r2, lp1), dot(p1, lp1)]
        parts += [dot(s, s), dot(s, r2), dot(s, p1), dot(r2, r2), dot(r2, p1), dot(p1, p1)]
        sol.append(s)
        dir1.append(p1)
        res2.append(r2)
        rr1s.append(rr1)
    for a in (sol[0], res2[0], dir1[0]):
        for b in (sol[1], res2[1], dir1[1]):
            parts.append(dot(a, b))
    sums = all_sum(1, parts)
    weights, final = [], []
    for v in range(2):
        r2lr2, r2lp1, p1lp1, ss, sr, sp, rr2, rp, pp = sums[9 * v : 9 * v + 9]
        beta1 = rr2 / rr1s[v]
        p2ap2 = (
            (rr2 + r2lr2) + 2.0 * beta1 * (rp + r2lp1) + beta1 * beta1 * (pp + p1lp1)
        )
        step2 = rr2 / p2ap2
        e, f = step2, step2 * beta1
        weights.append((e, f))
        final.append(
            ss + 2.0 * (e * sr + f * sp) + (e * e * rr2 + 2.0 * e * f * rp + f * f * pp)
        )
        for c in range(2):
            i = own[c]
            sout[v, col(c), :] = sol[v][i] + (e * res2[v][i] + f * dir1[v][i])
    cross_parts = sums[18:]
    (e0, f0), (e1, f1) = weights
    wa, wb = (None, e0, f0), (None, e1, f1)
    mix = cross_parts[0]
    for i in range(3):
        for j in range(3):
            if i == 0 and j == 0:
                continue
            term = cross_parts[3 * i + j]
            if wa[i] is not None:
                term = term * wa[i]
            if wb[j] is not None:
                term = term * wb[j]
            mix = mix + term
    count = float((levels + 1) * 2 * 8 * 128 * n)
    gram_one = (gram_t[0] + final[0]) / count
    gram_mix = (gram_t[1] + mix) / count
    gram_two = (gram_t[2] + final[1]) / count
    scale_one = jnp.sqrt(gram_one + EPSILON)
    cross = gram_mix / scale_one
    rest = gram_two - 2.0 * cross * cross + cross * cross * gram_one / (gram_one + EPSILON)
    scale_two = jnp.sqrt(rest + EPSILON)
    growth = jnp.where(lane == 0, scale_one, jnp.where(lane == 1, cross, scale_two))
    gout[...] = growth

    for g in range(len(chunks)):
        out_copy(g).wait()
        for side in range(2):
            a_copy(g, side).wait_send()
            b_copy(g, side).wait_send()
    for s in shifts:
        halo_copy(stat, st_send, st_recv, s).wait_send()
        halo_copy(ster, se_send, se_recv, s).wait_send()
    for turn in range(2):
        pltpu.make_async_copy(
            red.at[turn, pl.ds(0, n - 1)], red.at[turn, pl.ds(0, n - 1)], rd_send.at[turn]
        ).wait()


def finish(
    trc_hbm, surf_hbm, scales_hbm, out, sout, gout,
    trc, surf, scales, in_sem, buf, sbuf, gbuf, sem,
):
    levels = trc.shape[1]
    chunks = chunk_bounds(levels)
    scales_in = pltpu.make_async_copy(scales_hbm, scales, in_sem.at[0])
    surf_in = pltpu.make_async_copy(surf_hbm, surf, in_sem.at[1])
    scales_in.start()
    surf_in.start()
    ins = []
    for g, (k0, k1) in enumerate(chunks):
        ks = pl.ds(k0, k1 - k0)
        ins.append(pltpu.make_async_copy(trc_hbm.at[:, ks], trc.at[:, ks], in_sem.at[2 + g]))
        ins[-1].start()
    scales_in.wait()
    surf_in.wait()
    scale_one = scales[0:1, 0:1]
    cross = scales[0:1, 1:2]
    scale_two = scales[0:1, 2:3]
    inv_one, inv_two = 1.0 / scale_one, 1.0 / scale_two

    def pair(first, second):
        unit = first * inv_one
        return unit, (second - cross * unit) * inv_two

    sbuf[0], sbuf[1] = pair(surf[0], surf[1])
    gbuf[...] = scales[0:1, 0:3]
    copies = [
        pltpu.make_async_copy(sbuf, sout, sem.at[0]),
        pltpu.make_async_copy(gbuf, gout, sem.at[1]),
    ]
    for copy in copies:
        copy.start()
    for g, (k0, k1) in enumerate(chunks):

        def step(k, carry):
            buf[0, k], buf[1, k] = pair(trc[0, k], trc[1, k])
            return carry

        ins[g].wait()
        lax.fori_loop(k0, k1, step, 0, unroll=UNROLL)
        ks = pl.ds(k0, k1 - k0)
        copy = pltpu.make_async_copy(buf.at[:, ks], out.at[:, ks], sem.at[2 + g])
        copy.start()
        copies.append(copy)
    for copy in copies:
        copy.wait()


def packed(x):
    lead, (cols, rows) = x.shape[:-2], x.shape[-2:]
    x = x.reshape(lead + (cols, rows // 128, 128))
    x = jnp.swapaxes(x, -3, -2)
    return x.reshape(lead + (cols * (rows // 128), 128))


def unpacked(x, cols):
    lead, (rows, lanes) = x.shape[:-2], x.shape[-2:]
    x = x.reshape(lead + (rows // cols, cols, lanes))
    x = jnp.swapaxes(x, -3, -2)
    return x.reshape(lead + (cols, rows // cols * lanes))


def on_device(n, tracer_pert, surface_pert, zonal_flow, merid_flow, bottom_level):
    vectors, levels, columns, rows = tracer_pert.shape
    count = len(chunk_bounds(levels))
    f32 = jnp.float32
    vmem = pl.BlockSpec(memory_space=pltpu.VMEM)
    dma = pltpu.SemaphoreType.DMA
    slots = 2 * REACH + 1
    tracer, surface, tail = pl.pallas_call(
        functools.partial(kernel, n),
        out_shape=(
            jax.ShapeDtypeStruct((vectors, levels, 16, 128), f32),
            jax.ShapeDtypeStruct((vectors, 16, 128), f32),
            jax.ShapeDtypeStruct((8, 128), f32),
        ),
        in_specs=[pl.BlockSpec(memory_space=pltpu.HBM)] * 5,
        out_specs=(pl.BlockSpec(memory_space=pltpu.HBM), vmem, vmem),
        scratch_shapes=[
            pltpu.VMEM((vectors, levels, 16, 128), f32),
            dma((count,)),
            pltpu.VMEM((vectors, levels, 16, 128), f32),
            pltpu.VMEM((vectors, 16, 128), f32),
            pltpu.VMEM((levels, 16, 128), f32),
            pltpu.VMEM((levels, 16, 128), f32),
            pltpu.VMEM((16, 128), jnp.int32),
            dma((count, 2)),
            dma((3,)),
            pltpu.VMEM((2, levels, 3, 8, 128), f32),
            pltpu.VMEM((2, levels, 3, 8, 128), f32),
            pltpu.VMEM((2, levels, 2, 8, 128), f32),
            pltpu.VMEM((2, levels, 2, 8, 128), f32),
            pltpu.VMEM((levels, 10, 8, 128), f32),
            pltpu.VMEM((slots, 6, 8, 128), f32),
            pltpu.VMEM((slots, 4, 8, 128), f32),
            pltpu.VMEM((2, 1, 128), f32),
            pltpu.VMEM((2, n, 1, 128), f32),
            dma((2, count)),
            dma((2, count)),
            dma((2, count)),
            dma((2, count)),
            dma((slots,)),
            dma((slots,)),
            dma((slots,)),
            dma((slots,)),
            dma((2,)),
            dma((2,)),
        ],
        compiler_params=pltpu.CompilerParams(
            collective_id=0, has_side_effects=True, vmem_limit_bytes=67043328
        ),
    )(
        packed(tracer_pert),
        packed(surface_pert),
        packed(zonal_flow),
        packed(merid_flow),
        packed(bottom_level),
    )
    hbm = pl.BlockSpec(memory_space=pltpu.HBM)
    tracer_vec, surface_vec, growth = pl.pallas_call(
        finish,
        out_shape=(
            jax.ShapeDtypeStruct((vectors, levels, 16, 128), f32),
            jax.ShapeDtypeStruct((vectors, 16, 128), f32),
            jax.ShapeDtypeStruct((1, 3), f32),
        ),
        in_specs=[hbm] * 3,
        out_specs=(hbm,) * 3,
        scratch_shapes=[
            pltpu.VMEM((vectors, levels, 16, 128), f32),
            pltpu.VMEM((vectors, 16, 128), f32),
            pltpu.VMEM((8, 128), f32),
            dma((2 + count,)),
            pltpu.VMEM((vectors, levels, 16, 128), f32),
            pltpu.VMEM((vectors, 16, 128), f32),
            pltpu.VMEM((1, 3), f32),
            dma((2 + count,)),
        ],
        compiler_params=pltpu.CompilerParams(vmem_limit_bytes=67043328),
    )(tracer, surface, tail)
    return unpacked(tracer_vec, columns), unpacked(surface_vec, columns), growth.reshape(3)


def solution(mesh):
    placed = (
        P("grp", None, "lon", None),
        P("grp", "lon", None),
        P(None, "lon", None),
        P(None, "lon", None),
        P("lon", None),
    )
    return jax.shard_map(
        functools.partial(on_device, mesh.shape["lon"]),
        mesh=mesh,
        in_specs=placed,
        out_specs=(P("grp", None, "lon", None), P("grp", "lon", None), P("grp")),
        check_vma=False,
    )
```

```python
import functools

import jax
import jax.numpy as jnp
from jax import lax
from jax.experimental import pallas as pl
from jax.experimental.pallas import tpu as pltpu
from jax.sharding import PartitionSpec as P

DIFFUSIVITY = 0.5
TIME_STEP = 0.2
SURFACE_COUPLING = 0.5
STERIC_GAIN = 2.0
EPSILON = 1e-06
MESH = pl.DeviceIdType.MESH
CHUNK_EDGES = (0, 34, 64, 88, 100)
UNROLL = 5
REACH = 2


def chunk_bounds(levels):
    edges = sorted({levels * part // 100 for part in CHUNK_EDGES})
    return list(zip(edges[:-1], edges[1:]))


def peers_loop(n, body):
    if n <= 16:
        for i in range(1, n):
            body(i)
    else:

        def step(i, carry):
            body(i)
            return carry

        lax.fori_loop(1, n, step, 0)


def kernel(
    n, trc_hbm, surf_hbm, zon_hbm, mer_hbm, bot_hbm, out_hbm, sout, gout,
    out, out_sem, trc, surf, zon, mer, bot, in_sem, few_sem, s_a, r_a, s_b, r_b, coef, stat, ster, pack, red,
    a_send, a_recv, b_send, b_recv, st_send, st_recv, se_send, se_recv, rd_send, rd_recv,
):
    me = lax.axis_index("lon")
    levels = zon_hbm.shape[0]
    chunks = chunk_bounds(levels)
    right, left = lax.rem(me + 1, n), lax.rem(me + n - 1, n)
    side_dev = (left, right)
    tile = (8, 128)
    lane = lax.broadcasted_iota(jnp.int32, tile, 1)
    row = lax.broadcasted_iota(jnp.int32, tile, 0)
    last_lane, first_lane = lane == 127, lane == 0

    def north(x):
        rolled = pltpu.roll(x, 127, 1)
        return jnp.where(last_lane, pltpu.roll(rolled, 7, 0), rolled)

    def south(x):
        rolled = pltpu.roll(x, 1, 1)
        return jnp.where(first_lane, pltpu.roll(rolled, 1, 0), rolled)

    def col(c):
        return pl.ds(c, 8, stride=2)

    barrier = pltpu.get_barrier_semaphore()

    def greet(i):
        pl.semaphore_signal(
            barrier, inc=1, device_id={"lon": lax.rem(me + i, n)}, device_id_type=MESH
        )

    peers_loop(n, greet)

    def in_copies(g):
        k0, k1 = chunks[g]
        ks = pl.ds(k0, k1 - k0)
        return (
            pltpu.make_async_copy(trc_hbm.at[:, ks], trc.at[:, ks], in_sem.at[g, 0]),
            pltpu.make_async_copy(zon_hbm.at[ks], zon.at[ks], in_sem.at[g, 1]),
        )

    def out_copy(g):
        k0, k1 = chunks[g]
        ks = pl.ds(k0, k1 - k0)
        return pltpu.make_async_copy(out.at[:, ks], out_hbm.at[:, ks], out_sem.at[g])

    bot_in = pltpu.make_async_copy(bot_hbm, bot, few_sem.at[0])
    surf_in = pltpu.make_async_copy(surf_hbm, surf, few_sem.at[1])
    mer_in = pltpu.make_async_copy(mer_hbm, mer, few_sem.at[2])
    bot_in.start()
    surf_in.start()
    for copy in in_copies(0):
        copy.start()
    for g in range(1, len(chunks)):
        for copy in in_copies(g):
            copy.start()
    mer_in.start()

    def gather_chunk(g):
        for copy in in_copies(g):
            copy.wait()
        k0, k1 = chunks[g]

        def step(k, carry):
            for c in range(2):
                s_a[c, k, 0] = trc[0, k, col(c), :]
                s_a[c, k, 1] = trc[1, k, col(c), :]
                s_a[c, k, 2] = zon[k, col(c), :]
            return carry

        lax.fori_loop(k0, k1, step, 0, unroll=UNROLL)

    bot_in.wait()
    surf_in.wait()
    for c in range(2):
        d = bot[col(c), :].astype(jnp.float32)
        stat[REACH, 4 + c] = d
        for v in range(2):
            stat[REACH, 2 * v + c] = jnp.where(d > 0, surf[v, col(c), :], 0.0)

    def a_copy(g, side):
        k0, k1 = chunks[g]
        return pltpu.make_async_remote_copy(
            src_ref=s_a.at[side, pl.ds(k0, k1 - k0)],
            dst_ref=r_a.at[1 - side, pl.ds(k0, k1 - k0)],
            send_sem=a_send.at[side, g],
            recv_sem=a_recv.at[1 - side, g],
            device_id={"lon": side_dev[side]},
            device_id_type=MESH,
        )

    def b_copy(g, side):
        k0, k1 = chunks[g]
        return pltpu.make_async_remote_copy(
            src_ref=s_b.at[side, pl.ds(k0, k1 - k0)],
            dst_ref=r_b.at[1 - side, pl.ds(k0, k1 - k0)],
            send_sem=b_send.at[side, g],
            recv_sem=b_recv.at[1 - side, g],
            device_id={"lon": side_dev[side]},
            device_id_type=MESH,
        )

    shifts = [s for s in range(-REACH, REACH + 1) if s != 0]
    shifts.sort(key=abs)

    def halo_copy(buf, send, recv, s):
        return pltpu.make_async_remote_copy(
            src_ref=buf.at[REACH],
            dst_ref=buf.at[REACH - s],
            send_sem=send.at[REACH - s],
            recv_sem=recv.at[REACH - s],
            device_id={"lon": lax.rem(me + s + n, n)},
            device_id_type=MESH,
        )

    gather_chunk(0)
    pl.semaphore_wait(barrier, n - 1)
    for side in range(2):
        a_copy(0, side).start()
    for s in shifts:
        halo_copy(stat, st_send, st_recv, s).start()
    for g in range(1, len(chunks)):
        gather_chunk(g)
        for side in range(2):
            a_copy(g, side).start()

    for s in shifts[:2]:
        halo_copy(stat, st_send, st_recv, s).wait_recv()
    width = 2 * (2 * REACH + 1)
    mid = 2 * REACH

    def depth(i):
        return stat[i // 2, 4 + i % 2]

    def height(v, i):
        return stat[i // 2, 2 * v + i % 2]

    def y_face(i):
        d = depth(i)
        wall = jnp.logical_and(last_lane, row == 7)
        return jnp.where(wall, 0.0, jnp.minimum(d, north(d)))

    def x_face(i):
        return jnp.minimum(depth(i), depth(i + 1))

    half = TIME_STEP * 0.25
    diff = TIME_STEP * DIFFUSIVITY

    mer_in.wait()
    for g, (k0, k1) in enumerate(chunks):
        for side in range(2):
            a_copy(g, side).wait_recv()

        def first(k, carry):
            kf = k.astype(jnp.float32)
            z = (r_a[0, k, 2], s_a[0, k, 2], s_a[1, k, 2], r_a[1, k, 2])
            cx = []
            for f in range(3):
                open_f = kf < x_face(mid - 1 + f)
                u = half * (z[f] + z[f + 1])
                cx.append((jnp.where(open_f, u + diff, 0.0), jnp.where(open_f, u - diff, 0.0)))
            cy = []
            for c in range(2):
                open_f = kf < faces_y[c]
                m = mer[k, col(c), :]
                u = half * (m + north(m))
                cy.append((jnp.where(open_f, u + diff, 0.0), jnp.where(open_f, u - diff, 0.0)))
            for q, (lo, hi) in enumerate(cx + cy):
                coef[k, 2 * q] = lo
                coef[k, 2 * q + 1] = hi
            wet = [kf < depth(mid + c) for c in range(2)]
            for v in range(2):
                t = (
                    r_a[0, k, v],
                    jnp.where(wet[0], s_a[0, k, v], 0.0),
                    jnp.where(wet[1], s_a[1, k, v], 0.0),
                    r_a[1, k, v],
                )
                fx = [cx[f][0] * t[f] + cx[f][1] * t[f + 1] for f in range(3)]
                for c in range(2):
                    fy = cy[c][0] * t[c + 1] + cy[c][1] * north(t[c + 1])
                    s_b[c, k, v] = t[c + 1] - ((fx[c + 1] - fx[c]) + (fy - south(fy)))
            return carry

        if g == 0:
            faces_y = [y_face(mid + c) for c in range(2)]
        lax.fori_loop(k0, k1, first, 0, unroll=UNROLL)
        for side in range(2):
            b_copy(g, side).start()

    for s in shifts[2:]:
        halo_copy(stat, st_send, st_recv, s).wait_recv()

    face_x = {i: SURFACE_COUPLING * x_face(i) for i in range(0, width - 1)}
    face_y = {i: SURFACE_COUPLING * y_face(i) for i in range(1, width - 1)}

    def lap(s, cols):
        gx = {i: face_x[i] * (s[i + 1] - s[i]) for i in range(cols[0] - 1, cols[-1] + 1)}
        res = {}
        for i in cols:
            gy = face_y[i] * (north(s[i]) - s[i])
            res[i] = -((gx[i] - gx[i - 1]) + (gy - south(gy)))
        return res

    lap_h = [
        lap({i: height(v, i) for i in range(width)}, range(1, width - 1)) for v in range(2)
    ]

    zero = jnp.zeros(tile, jnp.float32)
    totals = (zero,) * 7
    for g, (k0, k1) in enumerate(chunks):
        for side in range(2):
            b_copy(g, side).wait_recv()

        def second(k, carry):
            sums, grams = list(carry[:4]), list(carry[4:])
            cx = [(coef[k, 2 * f], coef[k, 2 * f + 1]) for f in range(3)]
            cy = [(coef[k, 6 + 2 * c], coef[k, 7 + 2 * c]) for c in range(2)]
            new = []
            for v in range(2):
                t = (r_b[0, k, v], s_b[0, k, v], s_b[1, k, v], r_b[1, k, v])
                fx = [cx[f][0] * t[f] + cx[f][1] * t[f + 1] for f in range(3)]
                for c in range(2):
                    fy = cy[c][0] * t[c + 1] + cy[c][1] * north(t[c + 1])
                    val = t[c + 1] - ((fx[c + 1] - fx[c]) + (fy - south(fy)))
                    out[v, k, col(c), :] = val
                    sums[2 * v + c] = sums[2 * v + c] + val
                    new.append(val)
            grams[0] = grams[0] + (new[0] * new[0] + new[1] * new[1])
            grams[1] = grams[1] + (new[0] * new[2] + new[1] * new[3])
            grams[2] = grams[2] + (new[2] * new[2] + new[3] * new[3])
            return tuple(sums + grams)

        totals = lax.fori_loop(k0, k1, second, totals, unroll=UNROLL)
        out_copy(g).start()

    for q in range(4):
        ster[REACH, q] = totals[q]
    for s in reversed(shifts):
        halo_copy(ster, se_send, se_recv, s).start()

    def total_of(x):
        return jnp.sum(jnp.sum(x, axis=1, keepdims=True), axis=0, keepdims=True)

    def red_copy(turn, i):
        return pltpu.make_async_remote_copy(
            src_ref=pack.at[turn],
            dst_ref=red.at[turn, me],
            send_sem=rd_send.at[turn],
            recv_sem=rd_recv.at[turn],
            device_id={"lon": lax.rem(me + i, n)},
            device_id_type=MESH,
        )

    def all_sum(turn, parts):
        mine = zero
        for q, part in enumerate(parts):
            mine = jnp.where(lane == q, total_of(part), mine)
        pack[turn] = mine[0:1]
        red[turn, me] = mine[0:1]
        peers_loop(n, lambda i: red_copy(turn, i).start())
        every = pltpu.make_async_copy(
            red.at[turn, pl.ds(0, n - 1)], red.at[turn, pl.ds(0, n - 1)], rd_recv.at[turn]
        )
        every.wait()
        terms = [red[turn, i] for i in range(n)]
        while len(terms) > 1:
            terms = [
                terms[i] + terms[i + 1] if i + 1 < len(terms) else terms[i]
                for i in range(0, len(terms), 2)
            ]
        return [terms[0][0:1, q : q + 1] for q in range(len(parts))]

    gram_parts = list(totals[4:])
    for s in shifts:
        halo_copy(ster, se_send, se_recv, s).wait_recv()

    own = (mid, mid + 1)

    def dot(a, b):
        return a[own[0]] * b[own[0]] + a[own[1]] * b[own[1]]

    gain = STERIC_GAIN / levels
    res, lres, llres, parts = [], [], [], []
    for v in range(2):
        r = {
            i: gain * ster[i // 2, 2 * v + i % 2] - lap_h[v][i] for i in range(1, width - 1)
        }
        lr = lap(r, range(2, width - 2))
        llr = lap(lr, range(own[0], own[1] + 1))
        res.append(r)
        lres.append(lr)
        parts += [dot(r, r), dot(r, lr), dot(lr, lr), dot(lr, llr)]
    sums = all_sum(0, parts + gram_parts)
    gram_t = sums[8:]

    sol, dir1, res2, rr1s, parts = [], [], [], [], []
    ldir1s = []
    for v in range(2):
        l0, l1, l2, l3 = sums[4 * v : 4 * v + 4]
        step0 = l0 / (l0 + l1)
        ratio = l1 / l0
        rr1 = step0 * step0 * jnp.maximum(l2 - l1 * ratio, 0.0)
        beta0 = rr1 / l0
        along = step0 * ratio + beta0
        p1ap1 = (
            along * along * (l0 + l1)
            - 2.0 * along * step0 * (l1 + l2)
            + step0 * step0 * (l2 + l3)
        )
        step1 = rr1 / p1ap1
        r, lr = res[v], lres[v]
        p1 = {i: along * r[i] - step0 * lr[i] for i in range(own[0] - 2, own[1] + 3)}
        lp1 = lap(p1, range(own[0] - 1, own[1] + 2))
        r2 = {
            i: step0 * (ratio * r[i] - lr[i]) - step1 * (p1[i] + lp1[i])
            for i in range(own[0] - 1, own[1] + 2)
        }
        lr2 = lap(r2, range(own[0], own[1] + 1))
        s = {i: height(v, i) + (step0 * r[i] + step1 * p1[i]) for i in own}
        parts += [dot(r2, lr2), dot(r2, lp1), dot(p1, lp1)]
        parts += [dot(s, s), dot(s, r2), dot(s, p1), dot(r2, r2), dot(r2, p1), dot(p1, p1)]
        sol.append(s)
        dir1.append(p1)
        res2.append(r2)
        rr1s.append(rr1)
    for a in (sol[0], res2[0], dir1[0]):
        for b in (sol[1], res2[1], dir1[1]):
            parts.append(dot(a, b))
    sums = all_sum(1, parts)
    weights, final = [], []
    for v in range(2):
        r2lr2, r2lp1, p1lp1, ss, sr, sp, rr2, rp, pp = sums[9 * v : 9 * v + 9]
        beta1 = rr2 / rr1s[v]
        p2ap2 = (
            (rr2 + r2lr2) + 2.0 * beta1 * (rp + r2lp1) + beta1 * beta1 * (pp + p1lp1)
        )
        step2 = rr2 / p2ap2
        e, f = step2, step2 * beta1
        weights.append((e, f))
        final.append(
            ss + 2.0 * (e * sr + f * sp) + (e * e * rr2 + 2.0 * e * f * rp + f * f * pp)
        )
        for c in range(2):
            i = own[c]
            sout[v, col(c), :] = sol[v][i] + (e * res2[v][i] + f * dir1[v][i])
    cross_parts = sums[18:]
    (e0, f0), (e1, f1) = weights
    wa, wb = (None, e0, f0), (None, e1, f1)
    mix = cross_parts[0]
    for i in range(3):
        for j in range(3):
            if i == 0 and j == 0:
                continue
            term = cross_parts[3 * i + j]
            if wa[i] is not None:
                term = term * wa[i]
            if wb[j] is not None:
                term = term * wb[j]
            mix = mix + term
    count = float((levels + 1) * 2 * 8 * 128 * n)
    gram_one = (gram_t[0] + final[0]) / count
    gram_mix = (gram_t[1] + mix) / count
    gram_two = (gram_t[2] + final[1]) / count
    scale_one = jnp.sqrt(gram_one + EPSILON)
    cross = gram_mix / scale_one
    rest = gram_two - 2.0 * cross * cross + cross * cross * gram_one / (gram_one + EPSILON)
    scale_two = jnp.sqrt(rest + EPSILON)
    growth = jnp.where(lane == 0, scale_one, jnp.where(lane == 1, cross, scale_two))
    gout[...] = growth

    for g in range(len(chunks)):
        out_copy(g).wait()
        for side in range(2):
            a_copy(g, side).wait_send()
            b_copy(g, side).wait_send()
    for s in shifts:
        halo_copy(stat, st_send, st_recv, s).wait_send()
        halo_copy(ster, se_send, se_recv, s).wait_send()
    for turn in range(2):
        pltpu.make_async_copy(
            red.at[turn, pl.ds(0, n - 1)], red.at[turn, pl.ds(0, n - 1)], rd_send.at[turn]
        ).wait()


def finish(
    trc_hbm, surf_hbm, scales_hbm, out, sout, gout,
    trc, surf, scales, in_sem, buf, sbuf, gbuf, sem,
):
    levels = trc.shape[1]
    chunks = chunk_bounds(levels)
    scales_in = pltpu.make_async_copy(scales_hbm, scales, in_sem.at[0])
    surf_in = pltpu.make_async_copy(surf_hbm, surf, in_sem.at[1])
    scales_in.start()
    surf_in.start()
    ins = []
    for g, (k0, k1) in enumerate(chunks):
        ks = pl.ds(k0, k1 - k0)
        ins.append(pltpu.make_async_copy(trc_hbm.at[:, ks], trc.at[:, ks], in_sem.at[2 + g]))
        ins[-1].start()
    scales_in.wait()
    surf_in.wait()
    scale_one = scales[0:1, 0:1]
    cross = scales[0:1, 1:2]
    scale_two = scales[0:1, 2:3]
    inv_one, inv_two = 1.0 / scale_one, 1.0 / scale_two

    def pair(first, second):
        unit = first * inv_one
        return unit, (second - cross * unit) * inv_two

    sbuf[0], sbuf[1] = pair(surf[0], surf[1])
    gbuf[...] = scales[0:1, 0:3]
    copies = [
        pltpu.make_async_copy(sbuf, sout, sem.at[0]),
        pltpu.make_async_copy(gbuf, gout, sem.at[1]),
    ]
    for copy in copies:
        copy.start()
    for g, (k0, k1) in enumerate(chunks):

        def step(k, carry):
            buf[0, k], buf[1, k] = pair(trc[0, k], trc[1, k])
            return carry

        ins[g].wait()
        lax.fori_loop(k0, k1, step, 0, unroll=UNROLL)
        ks = pl.ds(k0, k1 - k0)
        copy = pltpu.make_async_copy(buf.at[:, ks], out.at[:, ks], sem.at[2 + g])
        copy.start()
        copies.append(copy)
    for copy in copies:
        copy.wait()


def packed(x):
    lead, (cols, rows) = x.shape[:-2], x.shape[-2:]
    x = x.reshape(lead + (cols, rows // 128, 128))
    x = jnp.swapaxes(x, -3, -2)
    return x.reshape(lead + (cols * (rows // 128), 128))


def unpacked(x, cols):
    lead, (rows, lanes) = x.shape[:-2], x.shape[-2:]
    x = x.reshape(lead + (rows // cols, cols, lanes))
    x = jnp.swapaxes(x, -3, -2)
    return x.reshape(lead + (cols, rows // cols * lanes))


def on_device(n, tracer_pert, surface_pert, zonal_flow, merid_flow, bottom_level):
    vectors, levels, columns, rows = tracer_pert.shape
    count = len(chunk_bounds(levels))
    f32 = jnp.float32
    vmem = pl.BlockSpec(memory_space=pltpu.VMEM)
    dma = pltpu.SemaphoreType.DMA
    slots = 2 * REACH + 1
    tracer, surface, tail = pl.pallas_call(
        functools.partial(kernel, n),
        out_shape=(
            jax.ShapeDtypeStruct((vectors, levels, 16, 128), f32),
            jax.ShapeDtypeStruct((vectors, 16, 128), f32),
            jax.ShapeDtypeStruct((8, 128), f32),
        ),
        in_specs=[pl.BlockSpec(memory_space=pltpu.HBM)] * 5,
        out_specs=(pl.BlockSpec(memory_space=pltpu.HBM), vmem, vmem),
        scratch_shapes=[
            pltpu.VMEM((vectors, levels, 16, 128), f32),
            dma((count,)),
            pltpu.VMEM((vectors, levels, 16, 128), f32),
            pltpu.VMEM((vectors, 16, 128), f32),
            pltpu.VMEM((levels, 16, 128), f32),
            pltpu.VMEM((levels, 16, 128), f32),
            pltpu.VMEM((16, 128), jnp.int32),
            dma((count, 2)),
            dma((3,)),
            pltpu.VMEM((2, levels, 3, 8, 128), f32),
            pltpu.VMEM((2, levels, 3, 8, 128), f32),
            pltpu.VMEM((2, levels, 2, 8, 128), f32),
            pltpu.VMEM((2, levels, 2, 8, 128), f32),
            pltpu.VMEM((levels, 10, 8, 128), f32),
            pltpu.VMEM((slots, 6, 8, 128), f32),
            pltpu.VMEM((slots, 4, 8, 128), f32),
            pltpu.VMEM((2, 1, 128), f32),
            pltpu.VMEM((2, n, 1, 128), f32),
            dma((2, count)),
            dma((2, count)),
            dma((2, count)),
            dma((2, count)),
            dma((slots,)),
            dma((slots,)),
            dma((slots,)),
            dma((slots,)),
            dma((2,)),
            dma((2,)),
        ],
        compiler_params=pltpu.CompilerParams(
            collective_id=0, has_side_effects=True, vmem_limit_bytes=67043328
        ),
    )(
        packed(tracer_pert),
        packed(surface_pert),
        packed(zonal_flow),
        packed(merid_flow),
        packed(bottom_level),
    )
    hbm = pl.BlockSpec(memory_space=pltpu.HBM)
    tracer_vec, surface_vec, growth = pl.pallas_call(
        finish,
        out_shape=(
            jax.ShapeDtypeStruct((vectors, levels, 16, 128), f32),
            jax.ShapeDtypeStruct((vectors, 16, 128), f32),
            jax.ShapeDtypeStruct((1, 3), f32),
        ),
        in_specs=[hbm] * 3,
        out_specs=(hbm,) * 3,
        scratch_shapes=[
            pltpu.VMEM((vectors, levels, 16, 128), f32),
            pltpu.VMEM((vectors, 16, 128), f32),
            pltpu.VMEM((8, 128), f32),
            dma((2 + count,)),
            pltpu.VMEM((vectors, levels, 16, 128), f32),
            pltpu.VMEM((vectors, 16, 128), f32),
            pltpu.VMEM((1, 3), f32),
            dma((2 + count,)),
        ],
        compiler_params=pltpu.CompilerParams(vmem_limit_bytes=67043328),
    )(tracer, surface, tail)
    return unpacked(tracer_vec, columns), unpacked(surface_vec, columns), growth.reshape(3)


def solution(mesh):
    placed = (
        P("grp", None, "lon", None),
        P("grp", "lon", None),
        P(None, "lon", None),
        P(None, "lon", None),
        P("lon", None),
    )
    return jax.shard_map(
        functools.partial(on_device, mesh.shape["lon"]),
        mesh=mesh,
        in_specs=placed,
        out_specs=(P("grp", None, "lon", None), P("grp", "lon", None), P("grp")),
        check_vma=False,
    )
```
